256 devices in a mesh: src: 32 (over x, z_lo, y), hid: 8 (over z_hi, core).
Axes of the slice: x: 4, y: 4, z: 8 (z_hi: 4, z_lo: 2; z = z_hi * 2 + z_lo), core: 2. Of those that a mesh axis runs over, the one named last changes fastest.
Arguments:
- source_field: float32 [256, 2, 98, 128], P('src'), may hold values from -36 to 36
- hidden_gain: float32 [98], replicated, may hold values from 0.1 to 1.9
- enc_tiles: float32 [8192, 128, 128], P(('src', 'hid')), may hold values from -0.25 to 0.25
- enc_src_block: int32 [8192], P(('src', 'hid')), may hold values from 0 to 255, as said below
- enc_hid_block: int32 [8192], P(('src', 'hid')), may hold values from 0 to 255, as said below
- enc_count: int32 [256], P(('src', 'hid')), may hold values from 1 to 32, as said below
- dec_tiles: float32 [8192, 128, 128], P(('src', 'hid')), may hold values from -0.15625 to 0.15625
- dec_src_block: int32 [8192], P(('src', 'hid')), may hold values from 0 to 255, as said below
- dec_hid_block: int32 [8192], P(('src', 'hid')), may hold values from 0 to 255, as said below
- dec_count: int32 [256], P(('src', 'hid')), may hold values from 1 to 32, as said below
Outputs:
- returned: float32 [256, 2, 98, 128], P('src')
- channel_rms: float32 [98], replicated
The draws below stay inside these ranges and needn't reach their ends.
Inputs may be any that keep to these rules, and one draw needn't show every extreme that they name: `enc_src_block`: the 32 entries starting at (s * 8 + h) * 32 lie in s * 8 to (s + 1) * 8 - 1. `enc_hid_block`: the 32 entries starting at (s * 8 + h) * 32 lie in h * 32 to (h + 1) * 32 - 1; within these entries no pair (enc_src_block, enc_hid_block) repeats. `enc_count`: entry s * 8 + h counts the live slots of that group; it equals 32 for some group. `dec_src_block`: the 32 entries starting at (s * 8 + h) * 32 lie in s * 8 to (s + 1) * 8 - 1. `dec_hid_block`: the 32 entries starting at (s * 8 + h) * 32 lie in h * 32 to (h + 1) * 32 - 1; within these entries no pair (dec_src_block, dec_hid_block) repeats. `dec_count`: entry s * 8 + h counts the live slots of that group; it equals 32 for some group.
All inputs are finite; a program needn't handle non-finite values.
Results may differ from the reference program's by a relative error of at most 0.0003.
Values sent between devices are 32-bit elements; how exact they have to be, the bound alone decides.
A program may use at most 64 MiB of HBM per device.

```python
import math
import jax
import jax.numpy as jnp
from jax import lax

CH = 98
BATCH = 2
TILE = 128
SRC_BLK = 8
HID_BLK = 32
ENC_CAP = 32
DEC_CAP = 32
SRC_BLOCKS = 256
HID_BLOCKS = 256
N_SRC = 32
N_HID = 8
DEVICES = 256


def block_pairs(key, salt, capacity):
    keys = jax.random.split(jax.random.fold_in(key, salt), DEVICES)

    def shuffle(one_key):
        return jax.random.permutation(one_key, SRC_BLK * HID_BLK)
    order = jax.vmap(shuffle)(keys)[:, :capacity].astype(jnp.int32)
    device = jnp.arange(DEVICES, dtype=jnp.int32)[:, None]
    src_base = device // N_HID * SRC_BLK
    hid_base = device % N_HID * HID_BLK
    return ((src_base + order // HID_BLK).reshape(-1), (hid_base + order % HID_BLK).reshape(-1))


def tile_counts(key, salt, capacity):
    first, second, third = jax.random.split(jax.random.fold_in(key, salt), 3)
    device = jnp.arange(DEVICES, dtype=jnp.int32)
    src_index = device // N_HID
    edge = max(1, N_SRC // 8)
    polar = (src_index < edge) | (src_index >= N_SRC - edge)
    heavy = jax.random.randint(first, (DEVICES,), capacity // 2, capacity + 1)
    light = jax.random.randint(second, (DEVICES,), 1, capacity // 4 + 1)
    counts = jnp.where(polar, heavy, light)
    fullest = jax.random.randint(third, (), 0, DEVICES)
    return counts.at[fullest].set(capacity).astype(jnp.int32)


def draw_source_field(key, part):
    first, second = jax.random.split(key, 2)
    shape = (SRC_BLOCKS, BATCH, CH, TILE)
    position = jnp.arange(SRC_BLOCKS, dtype=jnp.float32) / max(SRC_BLOCKS - 1, 1)
    channel = jnp.exp(jax.random.uniform(second, (CH,), jnp.float32, math.log(0.3), math.log(3.0)))
    ramp = 0.3 * 10.0 ** position
    noise = jnp.clip(jax.random.normal(first, shape, jnp.float32), -4.0, 4.0)
    return ramp[:, None, None, None] * channel[None, None, :, None] * noise


def draw_enc_src_block(key, part):
    return block_pairs(key, 11, ENC_CAP)[0]


def draw_enc_hid_block(key, part):
    return block_pairs(key, 11, ENC_CAP)[1]


def draw_enc_count(key, part):
    return tile_counts(key, 31, ENC_CAP)


def draw_dec_src_block(key, part):
    return block_pairs(key, 23, DEC_CAP)[0]


def draw_dec_hid_block(key, part):
    return block_pairs(key, 23, DEC_CAP)[1]


def draw_dec_count(key, part):
    return tile_counts(key, 37, DEC_CAP)


def steps_of(key, extent, cuts, smallest, largest):
    level = 1.0
    for dim, parts in cuts:
        heights = jax.random.uniform(jax.random.fold_in(jax.random.fold_in(key, 6), dim), (parts,), jnp.float32, smallest / len(cuts), largest / len(cuts))
        level = level * jnp.repeat(jnp.exp(heights), extent[dim] // parts).reshape((-1,) + (1,) * (len(extent) - 1 - dim))
    return level


def centred(key, extent, scale, limit, cuts=(), held_as=jnp.bfloat16):
    entries = scale * jax.random.normal(key, extent, jnp.float32)
    if cuts:
        entries = entries * steps_of(key, extent, cuts, -0.22, 0.18)
    return jnp.clip(entries, -limit, limit).astype(held_as)


def setup_inputs(seed: int = 0) -> dict:
    key_list = jax.random.split(jax.random.key(seed), 11)
    source_field = draw_source_field(jax.random.fold_in(key_list[10], 71), 0)
    hidden_gain = jnp.clip(1.0 + 0.18 * jax.random.normal(key_list[1], (CH,), jnp.float32), 0.1, 1.9)
    enc_tiles = centred(key_list[2], (DEVICES * ENC_CAP, TILE, TILE), (4 * TILE) ** -0.5, 0.25, ((0, 256),), jnp.float32)
    enc_src_block = draw_enc_src_block(jax.random.fold_in(key_list[10], 71), 0)
    enc_hid_block = draw_enc_hid_block(jax.random.fold_in(key_list[10], 71), 0)
    enc_count = draw_enc_count(jax.random.fold_in(key_list[10], 71), 0)
    dec_tiles = centred(key_list[6], (DEVICES * DEC_CAP, TILE, TILE), (12 * TILE) ** -0.5, 0.15625, ((0, 256),), jnp.float32)
    dec_src_block = draw_dec_src_block(jax.random.fold_in(key_list[10], 71), 0)
    dec_hid_block = draw_dec_hid_block(jax.random.fold_in(key_list[10], 71), 0)
    dec_count = draw_dec_count(jax.random.fold_in(key_list[10], 71), 0)
    return {"source_field": source_field, "hidden_gain": hidden_gain, "enc_tiles": enc_tiles, "enc_src_block": enc_src_block, "enc_hid_block": enc_hid_block, "enc_count": enc_count, "dec_tiles": dec_tiles, "dec_src_block": dec_src_block, "dec_hid_block": dec_hid_block, "dec_count": dec_count}


HIGH = lax.Precision.HIGHEST

def remap(values, tiles, from_block, to_block, counts, out_blocks, capacity):
    slots = jnp.arange(capacity, dtype=jnp.int32)

    def one_device(total, inputs):
        tile_set, sources, targets, live_count = inputs
        blocks = jnp.take(values, sources, axis=0)
        product = jnp.einsum('tfr,trc->tfc', blocks, tile_set, precision=HIGH)
        keep = (slots < live_count).astype(values.dtype)
        return (total.at[targets].add(product * keep[:, None, None]), None)
    start = jnp.zeros((out_blocks, values.shape[1], values.shape[2]), values.dtype)
    inputs = (tiles.reshape(-1, capacity, tiles.shape[1], tiles.shape[2]), from_block.reshape(-1, capacity), to_block.reshape(-1, capacity), counts)
    total, unused = lax.scan(one_device, start, inputs)
    return total

def normalize(total, gain, batch, channels):
    nodes, features, width = total.shape
    grouped = total.reshape(nodes, batch, channels, width)
    mean_square = lax.optimization_barrier(jnp.mean(grouped * grouped, axis=2, keepdims=True))
    scaled = grouped * gain[None, None, :, None] * lax.rsqrt(mean_square + 1e-06)
    return scaled.reshape(nodes, features, width)

def reference(source_field, hidden_gain, enc_tiles, enc_src_block, enc_hid_block, enc_count, dec_tiles, dec_src_block, dec_hid_block, dec_count):
    blocks, batch, channels, width = source_field.shape
    flat = source_field.reshape(blocks, batch * channels, width)
    hidden_sum = remap(flat, enc_tiles, enc_src_block, enc_hid_block, enc_count, HID_BLOCKS, ENC_CAP)
    hidden = normalize(hidden_sum, hidden_gain, batch, channels)
    returned = remap(hidden, dec_tiles, dec_hid_block, dec_src_block, dec_count, SRC_BLOCKS, DEC_CAP)
    returned = returned.reshape(source_field.shape)
    difference = returned - source_field
    channel_rms = jnp.sqrt(lax.optimization_barrier(jnp.mean(difference * difference, axis=(0, 1, 3))) + 1e-06)
    return (returned, channel_rms)
```

```python
import jax
import jax.numpy as jnp
from jax import lax
from jax.experimental import pallas as pl
from jax.experimental.pallas import tpu as pltpu
from jax.sharding import Mesh
from jax.sharding import PartitionSpec as P

CH = 98
BATCH = 2
TILE = 128
SRC_BLK = 8
HID_BLK = 32
CAP = 32
TOTAL_POINTS = 256 * BATCH * TILE
EPSILON = 1e-06
AXES = ("src_0", "src_1", "src_2", "hid_0", "hid_1")
SRC = ("src_0", "src_1", "src_2")
SIZES = {"src_0": 4, "src_1": 2, "src_2": 4, "hid_0": 4, "hid_1": 2}
MESH = pl.DeviceIdType.MESH
TILE_DMAS = 4

X, Z, Y, ZH, CORE = AXES


def hidden_slot(block, batch):
    x, z, y = block >> 3, (block >> 2) & 1, block & 3
    if batch == 0:
        return x * 8 + y * 2 + z
    return y * 8 + x * 2 + z


def split_pair(value):
    high = value.astype(jnp.bfloat16)
    low = (value - high.astype(jnp.float32)).astype(jnp.bfloat16)
    return high, low


def stacked_tile(tile):
    high, low = split_pair(tile)
    row = jnp.concatenate([high, low], axis=1)
    return jnp.concatenate([row, row], axis=0)


def full_product(left, right):
    both = jnp.dot(left, right, preferred_element_type=jnp.float32)
    return both[:, :TILE] + both[:, TILE:]


def tile_copies(tiles, held, sems):
    part = CAP // TILE_DMAS
    return [
        pltpu.make_async_copy(
            tiles.at[pl.ds(i * part, part)], held.at[pl.ds(i * part, part)], sems.at[i]
        )
        for i in range(TILE_DMAS)
    ]


def encode_kernel(src_ref, hid_ref, count_ref, field, tiles, out, held, left, sems):
    copies = tile_copies(tiles, held, sems)
    for copy in copies:
        copy.start()
    for s in range(SRC_BLK):
        for b in range(BATCH):
            left[s, b] = jnp.concatenate(split_pair(field[s, b]), axis=1)
    for b in range(BATCH):

        @pl.loop(0, HID_BLK)
        def _(j):
            out[b, j] = jnp.zeros((CH, TILE), jnp.float32)

    for copy in copies:
        copy.wait()

    @pl.loop(0, count_ref[0])
    def _(k):
        s = src_ref[k] & (SRC_BLK - 1)
        t = hid_ref[k] & (HID_BLK - 1)
        right = stacked_tile(held[k])
        for b in range(BATCH):
            slot = hidden_slot(t, b)
            out[b, slot] = out[b, slot] + full_product(left[s, b], right)


def decode_kernel(src_ref, hid_ref, count_ref, hidden, tiles, out, held, sems):
    copies = tile_copies(tiles, held, sems)
    for copy in copies:
        copy.start()
    for s in range(SRC_BLK):
        for b in range(BATCH):
            out[s, b] = jnp.zeros((CH, TILE), jnp.float32)
    for copy in copies:
        copy.wait()

    @pl.loop(0, count_ref[0])
    def _(k):
        s = src_ref[k] & (SRC_BLK - 1)
        t = hid_ref[k] & (HID_BLK - 1)
        right = stacked_tile(held[k])
        for b in range(BATCH):
            left = jnp.concatenate(split_pair(hidden[b, hidden_slot(t, b)]), axis=1)
            out[s, b] = out[s, b] + full_product(left, right)


def shifted(axis, step):
    size = SIZES[axis]
    return lax.rem(lax.axis_index(axis) + (step + size), size)


class Sender:
    def __init__(self, send_sems, recv_sems):
        self.send_sems, self.recv_sems, self.count, self.sent = send_sems, recv_sems, 0, []

    def start(self, src, dst, where):
        i = self.count
        self.count += 1
        copy = pltpu.make_async_remote_copy(
            src_ref=src,
            dst_ref=dst,
            send_sem=self.send_sems.at[i],
            recv_sem=self.recv_sems.at[i],
            device_id=where,
            device_id_type=MESH,
        )
        copy.start()
        self.sent.append(copy)
        return copy

    def finish(self):
        for copy in self.sent:
            copy.wait_send()


def greet(peers):
    barrier = pltpu.get_barrier_semaphore()
    for peer in peers:
        pl.semaphore_signal(barrier, inc=1, device_id=peer, device_id_type=MESH)
    pl.semaphore_wait(barrier, len(peers))


class RingSum:
    def __init__(self, sender, axis, part, landed, total):
        self.s, self.axis, self.part, self.landed, self.total = sender, axis, part, landed, total

    def begin(self):
        s, axis, part, landed = self.s, self.axis, self.part, self.landed
        right, left = {axis: shifted(axis, 1)}, {axis: shifted(axis, -1)}
        opposite = shifted(axis, 2)
        self.r1 = s.start(part(opposite, 0), landed.at[0], right)
        self.l1 = s.start(part(opposite, 1), landed.at[1], left)
        self.r2 = s.start(part(right[axis], 1), landed.at[2], right)
        self.l2 = s.start(part(left[axis], 0), landed.at[3], left)

    def middle(self):
        s, axis, part, landed = self.s, self.axis, self.part, self.landed
        right, left = {axis: shifted(axis, 1)}, {axis: shifted(axis, -1)}
        self.r1.wait_recv()
        landed[0] = landed[0] + part(right[axis], 0)[...]
        self.r3 = s.start(landed.at[0], landed.at[4], right)
        self.l1.wait_recv()
        landed[1] = landed[1] + part(left[axis], 1)[...]
        self.l3 = s.start(landed.at[1], landed.at[5], left)

    def end(self):
        me = lax.axis_index(self.axis)
        self.r2.wait_recv()
        self.l2.wait_recv()
        landed, part = self.landed, self.part
        self.r3.wait_recv()
        self.total(0)[...] = (part(me, 0)[...] + landed[3]) + landed[4]
        self.l3.wait_recv()
        self.total(1)[...] = (part(me, 1)[...] + landed[2]) + landed[5]


class RingGather:
    def __init__(self, sender, axis, part):
        self.s, self.axis, self.part = sender, axis, part

    def begin(self):
        s, axis, part = self.s, self.axis, self.part
        me = lax.axis_index(axis)
        right, left = {axis: shifted(axis, 1)}, {axis: shifted(axis, -1)}
        self.r1 = s.start(part(me, 0), part(me, 0), right)
        self.l1 = s.start(part(me, 1), part(me, 1), left)
        self.r2 = s.start(part(me, 1), part(me, 1), right)
        self.l2 = s.start(part(me, 0), part(me, 0), left)

    def middle(self):
        s, axis, part = self.s, self.axis, self.part
        right, left = {axis: shifted(axis, 1)}, {axis: shifted(axis, -1)}
        self.r1.wait_recv()
        self.r3 = s.start(part(left[axis], 0), part(left[axis], 0), right)
        self.l1.wait_recv()
        self.l3 = s.start(part(right[axis], 1), part(right[axis], 1), left)

    def end(self):
        for copy in (self.r2, self.l2, self.r3, self.l3):
            copy.wait_recv()


def run_together(rings):
    for ring in rings:
        ring.begin()
    for ring in rings:
        ring.middle()
    for ring in rings:
        ring.end()


def hidden_kernel(
    partial, gain, out, first_in, first_sum, second_in, second_sum, last_in, send_sems, recv_sems
):
    greet(
        [{X: shifted(X, 1)}, {X: shifted(X, -1)}, {Y: shifted(Y, 1)}, {Y: shifted(Y, -1)}]
        + [{Z: shifted(Z, 1)}]
    )
    s = Sender(send_sems, recv_sems)
    colours = ((X, Y), (Y, X))
    z = lax.axis_index(Z)
    other = 1 - z

    def first_sums(b, axis):
        return RingSum(
            s,
            axis,
            lambda i, h: partial.at[b, pl.ds(i * 8 + h * 4, 4)],
            first_in.at[b],
            lambda h: first_sum.at[b, pl.ds(h * 4, 4)],
        )

    def second_sums(b, axis):
        return RingSum(
            s,
            axis,
            lambda i, h: first_sum.at[b, i * 2 + h],
            second_in.at[b],
            lambda h: second_sum.at[b, h],
        )

    run_together([first_sums(b, colours[b][0]) for b in range(BATCH)])
    run_together([second_sums(b, colours[b][1]) for b in range(BATCH)])
    swaps = [
        s.start(second_sum.at[b, other], last_in.at[b], {Z: other}) for b in range(BATCH)
    ]
    rows = lax.broadcasted_iota(jnp.int32, (CH, CH), 0)
    columns = lax.broadcasted_iota(jnp.int32, (CH, CH), 1)
    scale = jnp.sum(
        jnp.where(rows == columns, jnp.broadcast_to(gain[...], (CH, CH)), 0.0),
        axis=1,
        keepdims=True,
    )
    pairs = []
    for b in range(BATCH):
        p, q = (lax.axis_index(axis) for axis in colours[b])
        swaps[b].wait_recv()
        value = second_sum[b, z] + last_in[b]
        mean_square = jnp.sum(value * value, axis=0, keepdims=True) * (1.0 / CH)
        slot = out.at[b, p * 8 + q * 2 + z]
        slot[...] = value * scale * lax.rsqrt(mean_square + EPSILON)
        pairs.append(s.start(slot, slot, {Z: other}))
    for pair in pairs:
        pair.wait_recv()

    def second_gather(b, axis):
        p = lax.axis_index(colours[b][0])
        return RingGather(s, axis, lambda i, h: out.at[b, p * 8 + i * 2 + h])

    def first_gather(b, axis):
        return RingGather(s, axis, lambda i, h: out.at[b, pl.ds(i * 8 + h * 4, 4)])

    run_together([second_gather(b, colours[b][1]) for b in range(BATCH)])
    run_together([first_gather(b, colours[b][0]) for b in range(BATCH)])
    s.finish()


def returned_kernel(
    partial, field, out, rms, core_in, core_sum, ring_in, squares, square_in, send_sems, recv_sems
):
    core = lax.axis_index(CORE)
    twin = 1 - core
    zh = lax.axis_index(ZH)
    z = lax.axis_index(Z)
    column = [
        (dz, dh, dc) for dz in range(2) for dh in range(4) for dc in range(2) if (dz, dh, dc) != (0, 0, 0)
    ]

    def stack_peer(dz, dh, dc):
        return {Z: lax.rem(z + dz, 2), ZH: lax.rem(zh + dh, 4), CORE: lax.rem(core + dc, 2)}

    lines = [{X: shifted(X, i)} for i in (1, 2, 3)], [{Y: shifted(Y, i)} for i in (1, 2, 3)]
    greet(lines[0] + lines[1] + [stack_peer(*step) for step in column])
    s = Sender(send_sems, recv_sems)
    order = [lax.rem(zh + i, 4) for i in (2, 1, 3, 0)]
    crossing = [
        s.start(partial.at[twin * 4 + i], core_in.at[i], {CORE: twin}) for i in order
    ]
    for i, copy in zip(order, crossing):
        copy.wait_recv()
        core_sum[i] = partial[core * 4 + i] + core_in[i]
    mine = out.at[core * 4 + zh]
    ring = RingSum(s, ZH, lambda i, h: core_sum.at[i, h], ring_in, lambda h: mine.at[h])
    run_together([ring])
    gather = RingGather(s, ZH, lambda i, h: out.at[core * 4 + i, h])
    gather.begin()
    error = mine[...] - field[core * 4 + zh]
    error = error * error
    column_sum = jnp.sum(error[0] + error[1], axis=1, keepdims=True)
    rows = lax.broadcasted_iota(jnp.int32, (CH, TILE), 0)
    columns = lax.broadcasted_iota(jnp.int32, (CH, TILE), 1)
    line = jnp.sum(jnp.where(rows == columns, column_sum, 0.0), axis=0, keepdims=True)
    squares[0] = jnp.broadcast_to(line, (8, TILE))

    def exchange(stage, first, peers):
        copies = [
            s.start(squares.at[stage], square_in.at[first + i], peer)
            for i, peer in enumerate(peers)
        ]
        return copies

    def collect(stage, first, copies):
        total = squares[stage]
        for i, copy in enumerate(copies):
            copy.wait_recv()
            total = total + square_in[first + i]
        squares[stage + 1] = total

    copies = exchange(0, 0, lines[0])
    gather.middle()
    collect(0, 0, copies)
    copies = exchange(1, 3, lines[1])
    swaps = [s.start(mine, mine, {CORE: twin})]
    collect(1, 3, copies)
    copies = exchange(2, 6, [stack_peer(*step) for step in column])
    gather.end()
    for i in (1, 2, 3):
        block = out.at[core * 4 + lax.rem(zh + i, 4)]
        swaps.append(s.start(block, block, {CORE: twin}))
    collect(2, 6, copies)
    rms[...] = jnp.sqrt(squares[3] * (1.0 / TOTAL_POINTS) + EPSILON)
    for copy in swaps:
        copy.wait_recv()
    s.finish()


VMEM = pl.BlockSpec(memory_space=pltpu.VMEM)
SMEM = pl.BlockSpec(memory_space=pltpu.SMEM)
ANY = pl.BlockSpec(memory_space=pl.ANY)


def f32(*shape):
    return jax.ShapeDtypeStruct(shape, jnp.float32)


def body(
    source_field,
    hidden_gain,
    enc_tiles,
    enc_src_block,
    enc_hid_block,
    enc_count,
    dec_tiles,
    dec_src_block,
    dec_hid_block,
    dec_count,
):
    held = pltpu.VMEM((CAP, TILE, TILE), jnp.float32)
    block = (CH, TILE)
    partial = pl.pallas_call(
        encode_kernel,
        out_shape=f32(BATCH, HID_BLK, *block),
        in_specs=[SMEM, SMEM, SMEM, VMEM, ANY],
        out_specs=VMEM,
        scratch_shapes=[
            held,
            pltpu.VMEM((SRC_BLK, BATCH, CH, 2 * TILE), jnp.bfloat16),
            pltpu.SemaphoreType.DMA((TILE_DMAS,)),
        ],
    )(enc_src_block, enc_hid_block, enc_count, source_field, enc_tiles)
    hidden = pl.pallas_call(
        hidden_kernel,
        out_shape=f32(BATCH, HID_BLK, *block),
        in_specs=[VMEM, VMEM],
        out_specs=VMEM,
        scratch_shapes=[
            pltpu.VMEM((BATCH, 6, 4, *block), jnp.float32),
            pltpu.VMEM((BATCH, 8, *block), jnp.float32),
            pltpu.VMEM((BATCH, 6, *block), jnp.float32),
            pltpu.VMEM((BATCH, 2, *block), jnp.float32),
            pltpu.VMEM((BATCH, *block), jnp.float32),
            pltpu.SemaphoreType.DMA((52,)),
            pltpu.SemaphoreType.DMA((52,)),
        ],
        compiler_params=pltpu.CompilerParams(collective_id=0, has_side_effects=True),
    )(partial, hidden_gain.reshape(1, CH))
    partial_back = pl.pallas_call(
        decode_kernel,
        out_shape=f32(SRC_BLK, BATCH, *block),
        in_specs=[SMEM, SMEM, SMEM, VMEM, ANY],
        out_specs=VMEM,
        scratch_shapes=[held, pltpu.SemaphoreType.DMA((TILE_DMAS,))],
    )(dec_src_block, dec_hid_block, dec_count, hidden, dec_tiles)
    returned, rms = pl.pallas_call(
        returned_kernel,
        out_shape=(f32(SRC_BLK, BATCH, *block), f32(8, TILE)),
        in_specs=[VMEM, VMEM],
        out_specs=(VMEM, VMEM),
        scratch_shapes=[
            pltpu.VMEM((4, BATCH, *block), jnp.float32),
            pltpu.VMEM((4, BATCH, *block), jnp.float32),
            pltpu.VMEM((6, *block), jnp.float32),
            pltpu.VMEM((4, 8, TILE), jnp.float32),
            pltpu.VMEM((21, 8, TILE), jnp.float32),
            pltpu.SemaphoreType.DMA((41,)),
            pltpu.SemaphoreType.DMA((41,)),
        ],
        compiler_params=pltpu.CompilerParams(collective_id=1, has_side_effects=True),
    )(partial_back, source_field)
    return returned, rms[0, :CH]


def solution(mesh):
    split = Mesh(mesh.devices.reshape(4, 2, 4, 4, 2), AXES)
    every = P(AXES)
    in_specs = (
        P(SRC, None, None, None),
        P(),
        P(AXES, None, None),
        every,
        every,
        every,
        P(AXES, None, None),
        every,
        every,
        every,
    )
    out_specs = (P(SRC, None, None, None), P())
    return jax.shard_map(body, mesh=split, in_specs=in_specs, out_specs=out_specs, check_vma=False)
```

```python
import jax
import jax.numpy as jnp
from jax import lax
from jax.experimental import pallas as pl
from jax.experimental.pallas import tpu as pltpu
from jax.sharding import Mesh
from jax.sharding import PartitionSpec as P

CH = 98
BATCH = 2
TILE = 128
ROWS = CH * BATCH
SRC_BLK = 8
HID_BLK = 32
CAP = 32
NONE = CAP
TOTAL_POINTS = 256 * BATCH * TILE
EPSILON = 1e-06
AXES = ("src_0", "src_1", "src_2", "hid_0", "hid_1")
SRC = ("src_0", "src_1", "src_2")
SIZES = {"src_0": 4, "src_1": 2, "src_2": 4, "hid_0": 4, "hid_1": 2}
MESH = pl.DeviceIdType.MESH
TILE_DMAS = 4
UNROLL = 4
N_SEMS = 176

X, Z, Y, ZH, CORE = AXES
CUTS = ((0, 96), (96, 100))
COLOURS = ((X, Y), (Y, X))


def slot_of(block, colour):
    x, z, y = block >> 3, (block >> 2) & 1, block & 3
    if colour == 0:
        return x * 8 + y * 2 + z
    return y * 8 + x * 2 + z


def block_in(slot, colour):
    p, q, z = slot >> 3, (slot >> 1) & 3, slot & 1
    if colour == 0:
        return p * 8 + z * 4 + q
    return q * 8 + z * 4 + p


def split_pair(value):
    high = value.astype(jnp.bfloat16)
    low = (value - high.astype(jnp.float32)).astype(jnp.bfloat16)
    return jnp.concatenate([high, low], axis=1)


def stacked_tile(tile):
    row = split_pair(tile)
    return jnp.concatenate([row, row], axis=0)


def full_product(left, right):
    both = jnp.dot(left, right, preferred_element_type=jnp.float32)
    return both[:, :TILE] + both[:, TILE:]


def tile_copies(tiles, held, sems):
    part = CAP // TILE_DMAS
    return [
        pltpu.make_async_copy(
            tiles.at[pl.ds(i * part, part)], held.at[pl.ds(i * part, part)], sems.at[i]
        )
        for i in range(TILE_DMAS)
    ]


def shifted(axis, step):
    size = SIZES[axis]
    return lax.rem(lax.axis_index(axis) + (step + size), size)


def chain(targets, count):
    row = lax.broadcasted_iota(jnp.int32, (CAP, CAP), 0)
    lane = lax.broadcasted_iota(jnp.int32, (CAP, CAP), 1)
    along = jnp.broadcast_to(targets, (CAP, CAP))
    down = jnp.sum(jnp.where(row == lane, along, 0), axis=1, keepdims=True)
    live = lane < count
    before = jnp.max(jnp.where(live & (lane < row) & (along == down), lane, -1), axis=1, keepdims=True)
    last = jnp.max(jnp.where(live & (along == row), lane, -1), axis=1, keepdims=True)
    return jnp.where(before < 0, NONE, before), jnp.where(last < 0, NONE, last)


class Sender:
    def __init__(self, send_sems, recv_sems):
        self.send_sems, self.recv_sems, self.count, self.sent = send_sems, recv_sems, 0, []

    def start(self, src, dst, where):
        i = self.count
        self.count += 1
        copy = pltpu.make_async_remote_copy(
            src_ref=src,
            dst_ref=dst,
            send_sem=self.send_sems.at[i],
            recv_sem=self.recv_sems.at[i],
            device_id=where,
            device_id_type=MESH,
        )
        copy.start()
        self.sent.append(copy)
        return copy

    def finish(self):
        for copy in self.sent:
            copy.wait_send()


class RingSum:
    def __init__(self, sender, axis, part, landed, total):
        self.s, self.axis, self.part, self.landed, self.total = sender, axis, part, landed, total
        self.right, self.left = {axis: shifted(axis, 1)}, {axis: shifted(axis, -1)}

    def begin_far(self):
        opposite = shifted(self.axis, 2)
        self.r1 = self.s.start(self.part(opposite, 0), self.landed(0), self.right)
        self.l1 = self.s.start(self.part(opposite, 1), self.landed(1), self.left)

    def begin_right(self):
        self.r2 = self.s.start(self.part(self.right[self.axis], 1), self.landed(2), self.right)

    def begin_left(self):
        self.l2 = self.s.start(self.part(self.left[self.axis], 0), self.landed(3), self.left)

    def begin(self):
        self.begin_far()
        self.begin_right()
        self.begin_left()

    def middle_right(self):
        self.r1.wait_recv()
        self.landed(0)[...] = self.landed(0)[...] + self.part(self.right[self.axis], 0)[...]
        self.r3 = self.s.start(self.landed(0), self.landed(4), self.right)

    def middle_left(self):
        self.l1.wait_recv()
        self.landed(1)[...] = self.landed(1)[...] + self.part(self.left[self.axis], 1)[...]
        self.l3 = self.s.start(self.landed(1), self.landed(5), self.left)

    def middle(self):
        self.middle_right()
        self.middle_left()

    def end(self):
        me = lax.axis_index(self.axis)
        landed, part = self.landed, self.part
        self.r2.wait_recv()
        self.l2.wait_recv()
        self.r3.wait_recv()
        self.total(0)[...] = (part(me, 0)[...] + landed(3)[...]) + landed(4)[...]
        self.l3.wait_recv()
        self.total(1)[...] = (part(me, 1)[...] + landed(2)[...]) + landed(5)[...]


class RingGather:
    def __init__(self, sender, axis, part):
        self.s, self.axis, self.part = sender, axis, part
        self.me = lax.axis_index(axis)
        self.right, self.left = {axis: shifted(axis, 1)}, {axis: shifted(axis, -1)}
        self.rights, self.lefts = [], []

    def give(self, half):
        mine = self.part(self.me, half)
        self.rights.append(self.s.start(mine, mine, self.right))
        self.lefts.append(self.s.start(mine, mine, self.left))


def whole_kernel(
    enc_src,
    enc_hid,
    enc_count,
    dec_src,
    dec_hid,
    dec_count,
    field,
    gain,
    enc_tiles,
    dec_tiles,
    out,
    rms,
    enc_held,
    dec_held,
    table,
    table_s,
    blocks,
    left,
    right,
    sums,
    partial_0,
    partial_1,
    first_in_0,
    first_in_1,
    first_sum_0,
    first_sum_1,
    second_in_0,
    second_in_1,
    second_sum_0,
    second_sum_1,
    last_in_0,
    last_in_1,
    hidden_0,
    hidden_1,
    back_0,
    back_1,
    core_in_0,
    core_in_1,
    core_sum_0,
    core_sum_1,
    ring_in_0,
    ring_in_1,
    result_0,
    result_1,
    squares,
    square_in,
    local_sems,
    send_sems,
    recv_sems,
):
    partial = (partial_0, partial_1)
    first_in, first_sum = (first_in_0, first_in_1), (first_sum_0, first_sum_1)
    second_in, second_sum = (second_in_0, second_in_1), (second_sum_0, second_sum_1)
    last_in, hidden = (last_in_0, last_in_1), (hidden_0, hidden_1)
    back, core_in, core_sum = (back_0, back_1), (core_in_0, core_in_1), (core_sum_0, core_sum_1)
    ring_in, result = (ring_in_0, ring_in_1), (result_0, result_1)
    both = (0, 1)
    x, y, z = lax.axis_index(X), lax.axis_index(Y), lax.axis_index(Z)
    zh, core = lax.axis_index(ZH), lax.axis_index(CORE)
    other, twin = 1 - z, 1 - core
    where = {X: x, Y: y}

    lines = [[{axis: shifted(axis, i)} for i in (1, 2, 3)] for axis in (X, Y)]
    stack = [
        {Z: lax.rem(z + dz, 2), ZH: lax.rem(zh + dh, 4), CORE: lax.rem(core + dc, 2)}
        for dz in range(2)
        for dh in range(4)
        for dc in range(2)
        if dz + dh + dc
    ]
    peers = lines[0] + lines[1] + stack
    barrier = pltpu.get_barrier_semaphore()
    for peer in peers:
        pl.semaphore_signal(barrier, inc=1, device_id=peer, device_id_type=MESH)

    enc_copies = tile_copies(enc_tiles, enc_held, local_sems.at[0])
    dec_copies = tile_copies(dec_tiles, dec_held, local_sems.at[1])
    for copy in enc_copies:
        copy.start()

    before, last = chain(enc_hid[...] & (HID_BLK - 1), enc_count[0])
    before_back, last_back = chain(dec_src[...] & (SRC_BLK - 1), dec_count[0])
    lane = lax.broadcasted_iota(jnp.int32, (CAP, TILE), 1)
    table[...] = jnp.where(
        lane == 0, before, jnp.where(lane == 1, last, jnp.where(lane == 2, before_back, last_back))
    )
    sums[NONE] = jnp.zeros((ROWS, TILE), jnp.float32)
    for s in range(SRC_BLK):
        value = field[s * ROWS : (s + 1) * ROWS]
        blocks[s] = value
        left[s] = split_pair(value)
    table_copy = pltpu.make_async_copy(table, table_s, local_sems.at[2, 0])
    table_copy.start()
    for copy in dec_copies:
        copy.start()
    table_copy.wait()
    for copy in enc_copies:
        copy.wait()

    @pl.loop(0, CAP // UNROLL)
    def _(step):
        for i in range(UNROLL):
            k = step * UNROLL + i
            product = full_product(left[enc_src[k] & (SRC_BLK - 1)], stacked_tile(enc_held[k]))
            sums[k] = sums[table_s[k, 0]] + product

    @pl.loop(0, HID_BLK)
    def _(slot):
        for c in both:
            start, rows = CUTS[c]
            partial[c][slot] = sums[table_s[block_in(slot, c), 1], start : start + rows]

    pl.semaphore_wait(barrier, len(peers))
    s = Sender(send_sems, recv_sems)

    order = (2, 1, 3, 0)

    def first_ring(c, i):
        p, q = COLOURS[c]
        there = shifted(q, order[i])
        return RingSum(
            s,
            p,
            lambda m, h: partial[c].at[m * 8 + there * 2 + h],
            lambda n: first_in[c].at[i, n],
            lambda h: first_sum[c].at[there * 2 + h],
        )

    first = [[first_ring(c, i) for i in range(4)] for c in both]
    second = [
        RingSum(
            s,
            COLOURS[c][1],
            lambda m, h, c=c: first_sum[c].at[m * 2 + h],
            lambda n, c=c: second_in[c].at[n],
            lambda h, c=c: second_sum[c].at[h],
        )
        for c in both
    ]
    for i in (0, 1):
        for c in both:
            first[c][i].begin()
    for copy in dec_copies:
        copy.wait()

    @pl.loop(0, CAP)
    def _(k):
        right[k] = stacked_tile(dec_held[k])

    def feed(c, i):
        ring = second[c]
        if i == 0:
            ring.begin_far()
        elif i == 1:
            ring.begin_right()
            ring.middle_right()
        elif i == 2:
            ring.begin_left()
            ring.middle_left()

    for i in range(4):
        for c in both:
            first[c][i].middle()
            if i + 2 < 4:
                first[c][i + 2].begin()
        if i >= 1:
            for c in both:
                first[c][i - 1].end()
                feed(c, i - 1)
    swaps = []
    for c in both:
        first[c][3].end()
        second[c].end()
        swaps.append(s.start(second_sum[c].at[other], last_in[c], {Z: other}))

    row = lax.broadcasted_iota(jnp.int32, (ROWS, CH), 0)
    column = lax.broadcasted_iota(jnp.int32, (ROWS, CH), 1)
    scale = jnp.sum(
        jnp.where((row >> 1) == column, jnp.broadcast_to(gain[...], (ROWS, CH)), 0.0),
        axis=1,
        keepdims=True,
    )
    values, evens, odds = [], [], []
    for c in both:
        swaps[c].wait_recv()
        value = second_sum[c][z] + last_in[c][...]
        values.append(value)
        parity = lax.broadcasted_iota(jnp.int32, value.shape, 0) & 1
        square = value * value
        evens.append(jnp.sum(jnp.where(parity == 0, square, 0.0), axis=0, keepdims=True))
        odds.append(jnp.sum(jnp.where(parity == 1, square, 0.0), axis=0, keepdims=True))
    even = lax.rsqrt((evens[0] + evens[1]) * (1.0 / CH) + EPSILON)
    odd = lax.rsqrt((odds[0] + odds[1]) * (1.0 / CH) + EPSILON)
    for c in both:
        start, rows = CUTS[c]
        parity = lax.broadcasted_iota(jnp.int32, (rows, TILE), 0) & 1
        p, q = (where[axis] for axis in COLOURS[c])
        hidden[c][p * 8 + q * 2 + z] = (
            values[c] * scale[start : start + rows] * jnp.where(parity == 0, even, odd)
        )

    def first_gather(c, step):
        p, q = COLOURS[c]
        there = shifted(q, step)
        return RingGather(s, p, lambda m, h: hidden[c].at[m * 8 + there * 2 + h])

    def second_gather(c):
        p, q = COLOURS[c]
        return RingGather(s, q, lambda m, h: hidden[c].at[where[p] * 8 + m * 2 + h])

    outer = [[first_gather(c, step) for step in (0, 3, 1, 2)] for c in both]
    inner = [second_gather(c) for c in both]
    pairs = []
    for c in both:
        mine = inner[c].part(inner[c].me, z)
        pairs.append(s.start(mine, mine, {Z: other}))
        inner[c].give(z)
    for c in both:
        outer[c][0].give(z)
    for c in both:
        pairs[c].wait_recv()
        inner[c].give(other)
    for c in both:
        outer[c][0].give(other)

    def arrive(ring):
        for copy in ring.rights + ring.lefts:
            copy.wait_recv()

    def forward(ring):
        far_right, far_left = ring.part(ring.left[ring.axis], 0), ring.part(ring.right[ring.axis], 1)
        ring.last = [s.start(far_right, far_right, ring.right), s.start(far_left, far_left, ring.left)]

    for c in both:
        arrive(inner[c])
        forward(inner[c])
        for ring in outer[c][1:3]:
            ring.give(0)
            ring.give(1)
    for c in both:
        arrive(outer[c][0])
        forward(outer[c][0])
    for c in both:
        for copy in inner[c].last:
            copy.wait_recv()
        outer[c][3].give(0)
        outer[c][3].give(1)
    for n in (1, 2, 3):
        for c in both:
            arrive(outer[c][n])
            forward(outer[c][n])
    for n in range(4):
        for c in both:
            for copy in outer[c][n].last:
                copy.wait_recv()

    @pl.loop(0, CAP // UNROLL)
    def _(step):
        for i in range(UNROLL):
            k = step * UNROLL + i
            block = dec_hid[k] & (HID_BLK - 1)
            pieces = [split_pair(hidden[c][slot_of(block, c)]) for c in both]
            product = full_product(jnp.concatenate(pieces, axis=0), right[k])
            sums[k] = sums[table_s[k, 2]] + product

    @pl.loop(0, SRC_BLK)
    def _(i):
        for c in both:
            start, rows = CUTS[c]
            back[c][i] = sums[table_s[i, 3], start : start + rows]

    crossing = {}
    for step in order:
        m = lax.rem(zh + step, 4)
        for c in both:
            crossing[step, c] = s.start(
                back[c].at[twin * 4 + m], core_in[c].at[m], {CORE: twin}
            )
    for step in order:
        m = lax.rem(zh + step, 4)
        for c in both:
            crossing[step, c].wait_recv()
            core_sum[c][m] = back[c][core * 4 + m] + core_in[c][m]
    column_ring = RingSum(
        s,
        ZH,
        lambda m, h: core_sum[h].at[m],
        lambda n: ring_in[(0, 1, 1, 0, 0, 1)[n]].at[(0, 0, 1, 1, 2, 2)[n]],
        lambda h: result[h].at[core * 4 + zh],
    )
    column_ring.begin()
    column_ring.middle()
    column_ring.end()

    gather = RingGather(s, ZH, lambda m, h: result[h].at[core * 4 + m])
    gather.give(0)
    gather.give(1)
    total = None
    for c in both:
        start, rows = CUTS[c]
        error = result[c][core * 4 + zh] - blocks[core * 4 + zh, start : start + rows]
        by_row = jnp.sum(error * error, axis=1, keepdims=True)
        row = start + lax.broadcasted_iota(jnp.int32, (rows, TILE), 0)
        column = lax.broadcasted_iota(jnp.int32, (rows, TILE), 1)
        part = jnp.sum(jnp.where((row >> 1) == column, by_row, 0.0), axis=0, keepdims=True)
        total = part if total is None else total + part
    squares[0] = jnp.broadcast_to(total, (8, TILE))

    def to_twin(m, c):
        block = result[c].at[core * 4 + m]
        return s.start(block, block, {CORE: twin})

    twins = [to_twin(zh, c) for c in both]

    def exchange(stage, first_slot, those):
        return [
            s.start(squares.at[stage], square_in.at[first_slot + i], peer)
            for i, peer in enumerate(those)
        ]

    def collect(stage, first_slot, copies):
        value = squares[stage]
        for i, copy in enumerate(copies):
            copy.wait_recv()
            value = value + square_in[first_slot + i]
        squares[stage + 1] = value

    copies = exchange(0, 0, lines[0])
    arrive(gather)
    forward(gather)
    collect(0, 0, copies)
    copies = exchange(1, 3, lines[1])
    for step in (1, 3):
        for c in both:
            twins.append(to_twin(lax.rem(zh + step, 4), c))
    collect(1, 3, copies)
    copies = exchange(2, 6, stack)
    for c, copy in zip(both, gather.last):
        copy.wait_recv()
        twins.append(to_twin(lax.rem(zh + 2, 4), c))
    collect(2, 6, copies)
    rms[...] = jnp.sqrt(squares[3] * (1.0 / TOTAL_POINTS) + EPSILON)
    for copy in twins:
        copy.wait_recv()
    for i in range(SRC_BLK):
        for c in both:
            start, rows = CUTS[c]
            out[i * ROWS + start : i * ROWS + start + rows] = result[c][i]
    s.finish()


VMEM = pl.BlockSpec(memory_space=pltpu.VMEM)
SMEM = pl.BlockSpec(memory_space=pltpu.SMEM)
ANY = pl.BlockSpec(memory_space=pl.ANY)


def coloured(*lead):
    return [pltpu.VMEM((*lead, rows, TILE), jnp.float32) for _, rows in CUTS]


def body(
    source_field,
    hidden_gain,
    enc_tiles,
    enc_src_block,
    enc_hid_block,
    enc_count,
    dec_tiles,
    dec_src_block,
    dec_hid_block,
    dec_count,
):
    rows = source_field.transpose(0, 2, 1, 3).reshape(SRC_BLK * ROWS, TILE)
    held = pltpu.VMEM((CAP, TILE, TILE), jnp.float32)
    returned, rms = pl.pallas_call(
        whole_kernel,
        out_shape=(
            jax.ShapeDtypeStruct((SRC_BLK * ROWS, TILE), jnp.float32),
            jax.ShapeDtypeStruct((8, TILE), jnp.float32),
        ),
        in_specs=[SMEM, VMEM, SMEM, VMEM, SMEM, SMEM, VMEM, VMEM, ANY, ANY],
        out_specs=(VMEM, VMEM),
        scratch_shapes=[
            held,
            held,
            pltpu.VMEM((CAP, TILE), jnp.int32),
            pltpu.SMEM((CAP, TILE), jnp.int32),
            pltpu.VMEM((SRC_BLK, ROWS, TILE), jnp.float32),
            pltpu.VMEM((SRC_BLK, ROWS, 2 * TILE), jnp.bfloat16),
            pltpu.VMEM((CAP, 2 * TILE, 2 * TILE), jnp.bfloat16),
            pltpu.VMEM((CAP + 1, ROWS, TILE), jnp.float32),
            *coloured(HID_BLK),
            *coloured(4, 6),
            *coloured(8),
            *coloured(6),
            *coloured(2),
            *coloured(),
            *coloured(HID_BLK),
            *coloured(SRC_BLK),
            *coloured(4),
            *coloured(4),
            *coloured(3),
            *coloured(SRC_BLK),
            pltpu.VMEM((4, 8, TILE), jnp.float32),
            pltpu.VMEM((21, 8, TILE), jnp.float32),
            pltpu.SemaphoreType.DMA((3, TILE_DMAS)),
            pltpu.SemaphoreType.DMA((N_SEMS,)),
            pltpu.SemaphoreType.DMA((N_SEMS,)),
        ],
        compiler_params=pltpu.CompilerParams(collective_id=0, has_side_effects=True),
    )(
        enc_src_block,
        enc_hid_block.reshape(1, CAP),
        enc_count,
        dec_src_block.reshape(1, CAP),
        dec_hid_block,
        dec_count,
        rows,
        hidden_gain.reshape(1, CH),
        enc_tiles,
        dec_tiles,
    )
    returned = returned.reshape(SRC_BLK, CH, BATCH, TILE).transpose(0, 2, 1, 3)
    return returned, rms[0, :CH]


def solution(mesh):
    split = Mesh(mesh.devices.reshape(4, 2, 4, 4, 2), AXES)
    every = P(AXES)
    in_specs = (
        P(SRC, None, None, None),
        P(),
        P(AXES, None, None),
        every,
        every,
        every,
        P(AXES, None, None),
        every,
        every,
        every,
    )
    out_specs = (P(SRC, None, None, None), P())
    return jax.shard_map(body, mesh=split, in_specs=in_specs, out_specs=out_specs, check_vma=False)
```

```python
import jax
import jax.numpy as jnp
from jax import lax
from jax.experimental import pallas as pl
from jax.experimental.pallas import tpu as pltpu
from jax.sharding import Mesh
from jax.sharding import PartitionSpec as P

CH = 98
BATCH = 2
TILE = 128
ROWS = CH * BATCH
SRC_BLK = 8
HID_BLK = 32
CAP = 32
NONE = CAP
TOTAL_POINTS = 256 * BATCH * TILE
EPSILON = 1e-06
AXES = ("src_0", "src_1", "src_2", "hid_0", "hid_1")
SRC = ("src_0", "src_1", "src_2")
SIZES = {"src_0": 4, "src_1": 2, "src_2": 4, "hid_0": 4, "hid_1": 2}
MESH = pl.DeviceIdType.MESH
TILE_DMAS = 4
UNROLL = 4
N_SEMS = 184
HALF = 48

X, Z, Y, ZH, CORE = AXES
CUTS = ((0, 96), (96, 100))
COLOURS = ((X, Y), (Y, X))


def slot_of(block, colour):
    x, z, y = block >> 3, (block >> 2) & 1, block & 3
    if colour == 0:
        return x * 8 + y * 2 + z
    return y * 8 + x * 2 + z


def block_in(slot, colour):
    p, q, z = slot >> 3, (slot >> 1) & 3, slot & 1
    if colour == 0:
        return p * 8 + z * 4 + q
    return q * 8 + z * 4 + p


def split_pair(value):
    high = value.astype(jnp.bfloat16)
    low = (value - high.astype(jnp.float32)).astype(jnp.bfloat16)
    return jnp.concatenate([high, low], axis=1)


def stacked_tile(tile):
    row = split_pair(tile)
    return jnp.concatenate([row, row], axis=0)


def full_product(left, right):
    both = jnp.dot(left, right, preferred_element_type=jnp.float32)
    return both[:, :TILE] + both[:, TILE:]


def tile_copies(tiles, held, sems):
    part = CAP // TILE_DMAS
    return [
        pltpu.make_async_copy(
            tiles.at[pl.ds(i * part, part)], held.at[pl.ds(i * part, part)], sems.at[i]
        )
        for i in range(TILE_DMAS)
    ]


def shifted(axis, step):
    size = SIZES[axis]
    return lax.rem(lax.axis_index(axis) + (step + size), size)


def chain(targets, count):
    row = lax.broadcasted_iota(jnp.int32, (CAP, CAP), 0)
    lane = lax.broadcasted_iota(jnp.int32, (CAP, CAP), 1)
    along = jnp.broadcast_to(targets, (CAP, CAP))
    down = jnp.sum(jnp.where(row == lane, along, 0), axis=1, keepdims=True)
    live = lane < jnp.broadcast_to(count, (CAP, CAP))
    before = jnp.max(jnp.where(live & (lane < row) & (along == down), lane, -1), axis=1, keepdims=True)
    last = jnp.max(jnp.where(live & (along == row), lane, -1), axis=1, keepdims=True)
    return jnp.where(before < 0, NONE, before), jnp.where(last < 0, NONE, last)


class Sender:
    def __init__(self, send_sems, recv_sems):
        self.send_sems, self.recv_sems, self.count, self.sent = send_sems, recv_sems, 0, []

    def start(self, src, dst, where):
        i = self.count
        self.count += 1
        copy = pltpu.make_async_remote_copy(
            src_ref=src,
            dst_ref=dst,
            send_sem=self.send_sems.at[i],
            recv_sem=self.recv_sems.at[i],
            device_id=where,
            device_id_type=MESH,
        )
        copy.start()
        self.sent.append(copy)
        return copy

    def finish(self):
        for copy in self.sent:
            copy.wait_send()


class RingSum:
    def __init__(self, sender, axis, part, landed, total):
        self.s, self.axis, self.part, self.landed, self.total = sender, axis, part, landed, total
        self.right, self.left = {axis: shifted(axis, 1)}, {axis: shifted(axis, -1)}

    def begin_far(self):
        opposite = shifted(self.axis, 2)
        self.r1 = self.s.start(self.part(opposite, 0), self.landed(0), self.right)
        self.l1 = self.s.start(self.part(opposite, 1), self.landed(1), self.left)

    def begin_right(self):
        self.r2 = self.s.start(self.part(self.right[self.axis], 1), self.landed(2), self.right)

    def begin_left(self):
        self.l2 = self.s.start(self.part(self.left[self.axis], 0), self.landed(3), self.left)

    def begin(self):
        self.begin_far()
        self.begin_right()
        self.begin_left()

    def middle_right(self):
        self.r1.wait_recv()
        self.landed(0)[...] = self.landed(0)[...] + self.part(self.right[self.axis], 0)[...]
        self.r3 = self.s.start(self.landed(0), self.landed(4), self.right)

    def middle_left(self):
        self.l1.wait_recv()
        self.landed(1)[...] = self.landed(1)[...] + self.part(self.left[self.axis], 1)[...]
        self.l3 = self.s.start(self.landed(1), self.landed(5), self.left)

    def middle(self):
        self.middle_right()
        self.middle_left()

    def end(self):
        me = lax.axis_index(self.axis)
        landed, part = self.landed, self.part
        self.r2.wait_recv()
        self.l2.wait_recv()
        self.r3.wait_recv()
        self.total(0)[...] = (part(me, 0)[...] + landed(3)[...]) + landed(4)[...]
        self.l3.wait_recv()
        self.total(1)[...] = (part(me, 1)[...] + landed(2)[...]) + landed(5)[...]


class RingGather:
    def __init__(self, sender, axis, part):
        self.s, self.axis, self.part = sender, axis, part
        self.me = lax.axis_index(axis)
        self.right, self.left = {axis: shifted(axis, 1)}, {axis: shifted(axis, -1)}
        self.rights, self.lefts = [], []

    def give(self, half):
        mine = self.part(self.me, half)
        self.rights.append(self.s.start(mine, mine, self.right))
        self.lefts.append(self.s.start(mine, mine, self.left))


def whole_kernel(
    enc_src_any,
    enc_hid_any,
    counts_any,
    dec_src_any,
    dec_hid_any,
    field_any,
    gain_any,
    enc_tiles,
    dec_tiles,
    result_0,
    result_1,
    rms,
    enc_src,
    enc_hid,
    counts,
    dec_src,
    dec_hid,
    field,
    gain,
    enc_held,
    dec_held,
    table,
    table_s,
    blocks,
    left,
    right,
    sums,
    partial_0,
    partial_1,
    first_in_0,
    first_in_1,
    first_sum_0,
    first_sum_1,
    pair_in_0,
    pair_in_1,
    pair_sum_0,
    pair_sum_1,
    second_in_0,
    second_in_1,
    second_sum_0,
    second_sum_1,
    hidden_0,
    hidden_1,
    back_0,
    back_1,
    core_in_0,
    core_in_1,
    core_sum_0,
    core_sum_1,
    ring_in_0,
    ring_in_1,
    squares,
    square_in,
    local_sems,
    send_sems,
    recv_sems,
):
    partial = (partial_0, partial_1)
    first_in, first_sum = (first_in_0, first_in_1), (first_sum_0, first_sum_1)
    pair_in, pair_sum = (pair_in_0, pair_in_1), (pair_sum_0, pair_sum_1)
    second_in, second_sum = (second_in_0, second_in_1), (second_sum_0, second_sum_1)
    hidden = (hidden_0, hidden_1)
    back, core_in, core_sum = (back_0, back_1), (core_in_0, core_in_1), (core_sum_0, core_sum_1)
    ring_in, result = (ring_in_0, ring_in_1), (result_0, result_1)
    both = (0, 1)
    x, y, z = lax.axis_index(X), lax.axis_index(Y), lax.axis_index(Z)
    zh, core = lax.axis_index(ZH), lax.axis_index(CORE)
    other, twin = 1 - z, 1 - core
    where = {X: x, Y: y}

    lines = [[{axis: shifted(axis, i)} for i in (1, 2, 3)] for axis in (X, Y)]
    stack = [
        {Z: lax.rem(z + dz, 2), ZH: lax.rem(zh + dh, 4), CORE: lax.rem(core + dc, 2)}
        for dz in range(2)
        for dh in range(4)
        for dc in range(2)
        if dz + dh + dc
    ]
    peers = lines[0] + lines[1] + stack
    barrier = pltpu.get_barrier_semaphore()
    small = [
        pltpu.make_async_copy(there, here, local_sems.at[2, i])
        for i, (there, here) in enumerate(
            (
                (enc_src_any, enc_src),
                (enc_hid_any, enc_hid),
                (counts_any, counts),
                (dec_src_any, dec_src),
                (dec_hid_any, dec_hid),
                (gain_any, gain),
            )
        )
    ]
    field_copy = pltpu.make_async_copy(field_any, field, local_sems.at[2, 7])
    enc_copies = tile_copies(enc_tiles, enc_held, local_sems.at[0])
    dec_copies = tile_copies(dec_tiles, dec_held, local_sems.at[1])
    for copy in (*small, field_copy, *enc_copies):
        copy.start()
    for peer in peers:
        pl.semaphore_signal(barrier, inc=1, device_id=peer, device_id_type=MESH)

    sums[NONE] = jnp.zeros((ROWS, TILE), jnp.float32)
    for copy in small:
        copy.wait()
    before, last = chain(enc_hid[...] & (HID_BLK - 1), counts[:, 0:1])
    before_back, last_back = chain(dec_src[...] & (SRC_BLK - 1), counts[:, 1:2])
    lane = lax.broadcasted_iota(jnp.int32, (CAP, TILE), 1)
    table[...] = jnp.where(
        lane == 0, before, jnp.where(lane == 1, last, jnp.where(lane == 2, before_back, last_back))
    )
    table_copy = pltpu.make_async_copy(table, table_s, local_sems.at[3, 0])
    field_copy.wait()
    for s in range(SRC_BLK):
        value = field[s * ROWS : (s + 1) * ROWS]
        blocks[s] = value
        left[s] = split_pair(value)
        if s == 1:
            table_copy.start()
    for copy in dec_copies:
        copy.start()
    table_copy.wait()
    for chunk, copy in enumerate(enc_copies):
        copy.wait()

        @pl.loop(0, CAP // TILE_DMAS // UNROLL)
        def _(step, chunk=chunk):
            for i in range(UNROLL):
                k = chunk * (CAP // TILE_DMAS) + step * UNROLL + i
                product = full_product(left[enc_src[k] & (SRC_BLK - 1)], stacked_tile(enc_held[k]))
                sums[k] = sums[table_s[k, 0]] + product

    @pl.loop(0, HID_BLK)
    def _(slot):
        for c in both:
            start, rows = CUTS[c]
            partial[c][slot] = sums[table_s[block_in(slot, c), 1], start : start + rows]

    pl.semaphore_wait(barrier, len(peers))
    s = Sender(send_sems, recv_sems)

    order = (2, 1, 3, 0)

    def first_ring(c, i):
        p, q = COLOURS[c]
        there = shifted(q, order[i])
        return RingSum(
            s,
            p,
            lambda m, h: partial[c].at[m * 8 + there * 2 + h],
            lambda n: first_in[c].at[i, n],
            lambda h: first_sum[c].at[there * 2 + h],
        )

    first = [[first_ring(c, i) for i in range(4)] for c in both]
    def part_rows(ref, h, rows):
        return ref.at[pl.ds(h * HALF, rows - HALF if h else HALF)]

    second = [
        RingSum(
            s,
            COLOURS[c][1],
            lambda m, h, c=c: part_rows(pair_sum[c].at[m], h, CUTS[c][1]),
            lambda n, c=c: second_in[c].at[
                n, pl.ds(0, CUTS[c][1] - HALF if n in (1, 2, 5) else HALF)
            ],
            lambda h, c=c: part_rows(second_sum[c], h, CUTS[c][1]),
        )
        for c in both
    ]
    pairs = {}

    def pair_out(c, i):
        there = shifted(COLOURS[c][1], order[i])
        pairs[c, i] = s.start(
            first_sum[c].at[there * 2 + other], pair_in[c].at[there], {Z: other}
        )

    def pair_back(c, i):
        there = shifted(COLOURS[c][1], order[i])
        pairs[c, i].wait_recv()
        pair_sum[c][there] = first_sum[c][there * 2 + z] + pair_in[c][there]

    for i in (0, 1):
        for c in both:
            first[c][i].begin()
    for copy in dec_copies:
        copy.wait()

    @pl.loop(0, CAP)
    def _(k):
        right[k] = stacked_tile(dec_held[k])

    def feed(c, i):
        ring = second[c]
        if i == 0:
            ring.begin_far()
        elif i == 1:
            ring.begin_right()
            ring.middle_right()
        elif i == 2:
            ring.begin_left()
            ring.middle_left()

    for i in range(4):
        for c in both:
            first[c][i].middle()
            if i + 2 < 4:
                first[c][i + 2].begin()
        if i >= 1:
            for c in both:
                first[c][i - 1].end()
                pair_out(c, i - 1)
        if i >= 2:
            for c in both:
                pair_back(c, i - 2)
                feed(c, i - 2)
    for c in both:
        first[c][3].end()
        pair_out(c, 3)
    for c in both:
        pair_back(c, 2)
        feed(c, 2)
    for c in both:
        pair_back(c, 3)
        second[c].end()

    row = lax.broadcasted_iota(jnp.int32, (ROWS, CH), 0)
    column = lax.broadcasted_iota(jnp.int32, (ROWS, CH), 1)
    scale = jnp.sum(
        jnp.where((row >> 1) == column, jnp.broadcast_to(gain[...], (ROWS, CH)), 0.0),
        axis=1,
        keepdims=True,
    )
    values, evens, odds = [], [], []
    for c in both:
        value = second_sum[c][...]
        values.append(value)
        parity = lax.broadcasted_iota(jnp.int32, value.shape, 0) & 1
        square = value * value
        evens.append(jnp.sum(jnp.where(parity == 0, square, 0.0), axis=0, keepdims=True))
        odds.append(jnp.sum(jnp.where(parity == 1, square, 0.0), axis=0, keepdims=True))
    even = lax.rsqrt((evens[0] + evens[1]) * (1.0 / CH) + EPSILON)
    odd = lax.rsqrt((odds[0] + odds[1]) * (1.0 / CH) + EPSILON)
    for c in both:
        start, rows = CUTS[c]
        parity = lax.broadcasted_iota(jnp.int32, (rows, TILE), 0) & 1
        p, q = (where[axis] for axis in COLOURS[c])
        hidden[c][p * 8 + q * 2 + z] = (
            values[c] * scale[start : start + rows] * jnp.where(parity == 0, even, odd)
        )

    def outer_block(c, m, step, far):
        there = shifted(COLOURS[c][1], step)
        return hidden[c].at[m * 8 + there * 2 + (other if far else z)]

    def inner_block(c, step):
        p, q = COLOURS[c]
        return hidden[c].at[where[p] * 8 + shifted(q, step) * 2 + z]

    def send(block, axis, step):
        return s.start(block, block, {axis: shifted(axis, step)})

    inner, paired, outer, passed = {}, {}, {}, {}

    def to_pair(c, step):
        paired[c, step] = send(inner_block(c, step), Z, 1)

    def to_line(c, step, far):
        p = COLOURS[c][0]
        block = outer_block(c, where[p], step, far)
        outer[c, step, far] = [send(block, p, 1), send(block, p, -1)]

    def along_line(c, step, far):
        p = COLOURS[c][0]
        from_left, from_right = outer[c, step, far]
        if far:
            from_right.wait_recv()
            passed[c, step, far] = send(outer_block(c, shifted(p, 1), step, far), p, -1)
        else:
            from_left.wait_recv()
            passed[c, step, far] = send(outer_block(c, shifted(p, -1), step, far), p, 1)

    def settle_line(c, step, far):
        outer[c, step, far][0 if far else 1].wait_recv()
        passed[c, step, far].wait_recv()

    for c in both:
        q, mine = COLOURS[c][1], inner_block(c, 0)
        inner[c] = [send(mine, q, 1), send(mine, q, -1)]
        to_pair(c, 0)
    for c in both:
        to_line(c, 0, False)
    for c in both:
        q, rows = COLOURS[c][1], CUTS[c][1]
        from_left, from_right = inner[c]
        from_left.wait_recv()
        inner[c] = [send(part_rows(inner_block(c, -1), 0, rows), q, 1)]
        to_pair(c, -1)
        from_right.wait_recv()
        inner[c].append(send(part_rows(inner_block(c, 1), 1, rows), q, -1))
        to_pair(c, 1)
        to_line(c, -1, False)
        to_line(c, 1, False)
    for c in both:
        paired[c, 0].wait_recv()
        to_line(c, 0, True)
    for c in both:
        along_line(c, 0, False)
    for c in both:
        for copy in inner[c]:
            copy.wait_recv()
        to_pair(c, 2)
        to_line(c, 2, False)
    for c in both:
        for step in (-1, 1):
            paired[c, step].wait_recv()
            to_line(c, step, True)
    for c in both:
        along_line(c, -1, False)
        along_line(c, 1, False)
        along_line(c, 0, True)
    for c in both:
        paired[c, 2].wait_recv()
        to_line(c, 2, True)
    for c in both:
        along_line(c, 2, False)
        along_line(c, -1, True)
        along_line(c, 1, True)
    for c in both:
        along_line(c, 2, True)
    for key in passed:
        settle_line(*key)

    @pl.loop(0, CAP // UNROLL)
    def _(step):
        for i in range(UNROLL):
            k = step * UNROLL + i
            block = dec_hid[k] & (HID_BLK - 1)
            pieces = [split_pair(hidden[c][slot_of(block, c)]) for c in both]
            product = full_product(jnp.concatenate(pieces, axis=0), right[k])
            sums[k] = sums[table_s[k, 2]] + product

    @pl.loop(0, SRC_BLK)
    def _(i):
        for c in both:
            start, rows = CUTS[c]
            back[c][i] = sums[table_s[i, 3], start : start + rows]

    crossing = {}
    for step in order:
        m = lax.rem(zh + step, 4)
        for c in both:
            crossing[step, c] = s.start(
                back[c].at[twin * 4 + m], core_in[c].at[m], {CORE: twin}
            )
    column_ring = RingSum(
        s,
        ZH,
        lambda m, h: core_sum[h].at[m],
        lambda n: ring_in[(0, 1, 1, 0, 0, 1)[n]].at[(0, 0, 1, 1, 2, 2)[n]],
        lambda h: result[h].at[core * 4 + zh],
    )
    for step in order:
        m = lax.rem(zh + step, 4)
        for c in both:
            crossing[step, c].wait_recv()
            core_sum[c][m] = back[c][core * 4 + m] + core_in[c][m]
        if step == 2:
            column_ring.begin_far()
        elif step == 1:
            column_ring.begin_right()
        elif step == 3:
            column_ring.begin_left()
    column_ring.middle()
    column_ring.end()

    def arrive(ring):
        for copy in ring.rights + ring.lefts:
            copy.wait_recv()

    def forward(ring):
        far_right, far_left = ring.part(ring.left[ring.axis], 0), ring.part(ring.right[ring.axis], 1)
        ring.last = [s.start(far_right, far_right, ring.right), s.start(far_left, far_left, ring.left)]

    gather = RingGather(s, ZH, lambda m, h: result[h].at[core * 4 + m])
    gather.give(0)
    gather.give(1)
    total = None
    for c in both:
        start, rows = CUTS[c]
        error = result[c][core * 4 + zh] - blocks[core * 4 + zh, start : start + rows]
        by_row = jnp.sum(error * error, axis=1, keepdims=True)
        row = start + lax.broadcasted_iota(jnp.int32, (rows, TILE), 0)
        column = lax.broadcasted_iota(jnp.int32, (rows, TILE), 1)
        part = jnp.sum(jnp.where((row >> 1) == column, by_row, 0.0), axis=0, keepdims=True)
        total = part if total is None else total + part
    squares[0] = jnp.broadcast_to(total, (8, TILE))

    def to_twin(m, c):
        block = result[c].at[core * 4 + m]
        return s.start(block, block, {CORE: twin})

    twins = [to_twin(zh, c) for c in both]

    def exchange(stage, first_slot, those):
        return [
            s.start(squares.at[stage], square_in.at[first_slot + i], peer)
            for i, peer in enumerate(those)
        ]

    def collect(stage, first_slot, copies):
        value = squares[stage]
        for i, copy in enumerate(copies):
            copy.wait_recv()
            value = value + square_in[first_slot + i]
        squares[stage + 1] = value

    copies = exchange(0, 0, lines[0])
    arrive(gather)
    forward(gather)
    collect(0, 0, copies)
    copies = exchange(1, 3, lines[1])
    for step in (1, 3):
        for c in both:
            twins.append(to_twin(lax.rem(zh + step, 4), c))
    collect(1, 3, copies)
    copies = exchange(2, 6, stack)
    for c, copy in zip(both, gather.last):
        copy.wait_recv()
        twins.append(to_twin(lax.rem(zh + 2, 4), c))
    collect(2, 6, copies)
    rms[...] = jnp.sqrt(squares[3] * (1.0 / TOTAL_POINTS) + EPSILON)
    for copy in twins:
        copy.wait_recv()
    s.finish()


def assemble_kernel(result_0, result_1, rms, out, rms_out):
    for i in range(SRC_BLK):
        for (start, rows), part in zip(CUTS, (result_0, result_1)):
            out[i * ROWS + start : i * ROWS + start + rows] = part[i]
    rms_out[...] = rms[0:1, 0:CH]


VMEM = pl.BlockSpec(memory_space=pltpu.VMEM)
HBM = pl.BlockSpec(memory_space=pltpu.HBM)


def coloured(*lead):
    return [pltpu.VMEM((*lead, rows, TILE), jnp.float32) for _, rows in CUTS]


def body(
    source_field,
    hidden_gain,
    enc_tiles,
    enc_src_block,
    enc_hid_block,
    enc_count,
    dec_tiles,
    dec_src_block,
    dec_hid_block,
    dec_count,
):
    rows = source_field.transpose(0, 2, 1, 3).reshape(SRC_BLK * ROWS, TILE)
    held = pltpu.VMEM((CAP, TILE, TILE), jnp.float32)
    pieces = pl.pallas_call(
        whole_kernel,
        out_shape=(*coloured(SRC_BLK), pltpu.VMEM((8, TILE), jnp.float32)),
        in_specs=[HBM] * 9,
        out_specs=(VMEM, VMEM, VMEM),
        scratch_shapes=[
            pltpu.SMEM((CAP,), jnp.int32),
            pltpu.VMEM((1, CAP), jnp.int32),
            pltpu.VMEM((1, 2), jnp.int32),
            pltpu.VMEM((1, CAP), jnp.int32),
            pltpu.SMEM((CAP,), jnp.int32),
            pltpu.VMEM((SRC_BLK * ROWS, TILE), jnp.float32),
            pltpu.VMEM((1, CH), jnp.float32),
            held,
            held,
            pltpu.VMEM((CAP, TILE), jnp.int32),
            pltpu.SMEM((CAP, TILE), jnp.int32),
            pltpu.VMEM((SRC_BLK, ROWS, TILE), jnp.float32),
            pltpu.VMEM((SRC_BLK, ROWS, 2 * TILE), jnp.bfloat16),
            pltpu.VMEM((CAP, 2 * TILE, 2 * TILE), jnp.bfloat16),
            pltpu.VMEM((CAP + 1, ROWS, TILE), jnp.float32),
            *coloured(HID_BLK),
            *coloured(4, 6),
            *coloured(8),
            *coloured(4),
            *coloured(4),
            *[pltpu.VMEM((6, 56, TILE), jnp.float32)] * 2,
            *coloured(),
            *coloured(HID_BLK),
            *coloured(SRC_BLK),
            *coloured(4),
            *coloured(4),
            *coloured(3),
            pltpu.VMEM((4, 8, TILE), jnp.float32),
            pltpu.VMEM((21, 8, TILE), jnp.float32),
            pltpu.SemaphoreType.DMA((4, 8)),
            pltpu.SemaphoreType.DMA((N_SEMS,)),
            pltpu.SemaphoreType.DMA((N_SEMS,)),
        ],
        compiler_params=pltpu.CompilerParams(collective_id=0, has_side_effects=True),
    )(
        enc_src_block,
        enc_hid_block.reshape(1, CAP),
        jnp.concatenate([enc_count, dec_count]).reshape(1, 2),
        dec_src_block.reshape(1, CAP),
        dec_hid_block,
        rows,
        hidden_gain.reshape(1, CH),
        enc_tiles,
        dec_tiles,
    )
    returned, rms = pl.pallas_call(
        assemble_kernel,
        out_shape=(
            jax.ShapeDtypeStruct((SRC_BLK * ROWS, TILE), jnp.float32),
            jax.ShapeDtypeStruct((1, CH), jnp.float32),
        ),
        in_specs=[VMEM] * 3,
        out_specs=(VMEM, VMEM),
    )(*[pltpu.with_memory_space_constraint(piece, pltpu.VMEM) for piece in pieces])
    returned = returned.reshape(SRC_BLK, CH, BATCH, TILE).transpose(0, 2, 1, 3)
    return returned, rms.reshape(CH)


def solution(mesh):
    split = Mesh(mesh.devices.reshape(4, 2, 4, 4, 2), AXES)
    every = P(AXES)
    in_specs = (
        P(SRC, None, None, None),
        P(),
        P(AXES, None, None),
        every,
        every,
        every,
        P(AXES, None, None),
        every,
        every,
        every,
    )
    out_specs = (P(SRC, None, None, None), P())
    return jax.shard_map(body, mesh=split, in_specs=in_specs, out_specs=out_specs, check_vma=False)
```

```python
import jax
import jax.numpy as jnp
from jax import lax
from jax.experimental import pallas as pl
from jax.experimental.pallas import tpu as pltpu
from jax.sharding import Mesh
from jax.sharding import PartitionSpec as P

CH = 98
BATCH = 2
TILE = 128
ROWS = CH * BATCH
SRC_BLK = 8
HID_BLK = 32
CAP = 32
NONE = CAP
TOTAL_POINTS = 256 * BATCH * TILE
EPSILON = 1e-06
AXES = ("src_0", "src_1", "src_2", "hid_0", "hid_1")
SRC = ("src_0", "src_1", "src_2")
SIZES = {"src_0": 4, "src_1": 2, "src_2": 4, "hid_0": 4, "hid_1": 2}
MESH = pl.DeviceIdType.MESH
TILE_DMAS = 4
UNROLL = 4
N_SEMS = 184
HALF = 48

X, Z, Y, ZH, CORE = AXES
CUTS = ((0, 96), (96, 100))
COLOURS = ((X, Y), (Y, X))


def slot_of(block, colour):
    x, z, y = block >> 3, (block >> 2) & 1, block & 3
    if colour == 0:
        return x * 8 + y * 2 + z
    return y * 8 + x * 2 + z


def block_in(slot, colour):
    p, q, z = slot >> 3, (slot >> 1) & 3, slot & 1
    if colour == 0:
        return p * 8 + z * 4 + q
    return q * 8 + z * 4 + p


def split_pair(value):
    high = value.astype(jnp.bfloat16)
    low = (value - high.astype(jnp.float32)).astype(jnp.bfloat16)
    return jnp.concatenate([high, low], axis=1)


def stacked_tile(tile):
    row = split_pair(tile)
    return jnp.concatenate([row, row], axis=0)


def full_product(left, right):
    both = jnp.dot(left, right, preferred_element_type=jnp.float32)
    return both[:, :TILE] + both[:, TILE:]


def tile_copies(tiles, held, sems):
    part = CAP // TILE_DMAS
    return [
        pltpu.make_async_copy(
            tiles.at[pl.ds(i * part, part)], held.at[pl.ds(i * part, part)], sems.at[i]
        )
        for i in range(TILE_DMAS)
    ]


def shifted(axis, step):
    size = SIZES[axis]
    return lax.rem(lax.axis_index(axis) + (step + size), size)


def chain(targets, count):
    row = lax.broadcasted_iota(jnp.int32, (CAP, CAP), 0)
    lane = lax.broadcasted_iota(jnp.int32, (CAP, CAP), 1)
    along = jnp.broadcast_to(targets, (CAP, CAP))
    down = jnp.sum(jnp.where(row == lane, along, 0), axis=1, keepdims=True)
    live = lane < count
    before = jnp.max(jnp.where(live & (lane < row) & (along == down), lane, -1), axis=1, keepdims=True)
    last = jnp.max(jnp.where(live & (along == row), lane, -1), axis=1, keepdims=True)
    return jnp.where(before < 0, NONE, before), jnp.where(last < 0, NONE, last)


class Sender:
    def __init__(self, send_sems, recv_sems):
        self.send_sems, self.recv_sems, self.count, self.sent = send_sems, recv_sems, 0, []

    def start(self, src, dst, where):
        i = self.count
        self.count += 1
        copy = pltpu.make_async_remote_copy(
            src_ref=src,
            dst_ref=dst,
            send_sem=self.send_sems.at[i],
            recv_sem=self.recv_sems.at[i],
            device_id=where,
            device_id_type=MESH,
        )
        copy.start()
        self.sent.append(copy)
        return copy

    def finish(self):
        for copy in self.sent:
            copy.wait_send()


class RingSum:
    def __init__(self, sender, axis, part, landed, total):
        self.s, self.axis, self.part, self.landed, self.total = sender, axis, part, landed, total
        self.right, self.left = {axis: shifted(axis, 1)}, {axis: shifted(axis, -1)}

    def begin_far(self):
        opposite = shifted(self.axis, 2)
        self.r1 = self.s.start(self.part(opposite, 0), self.landed(0), self.right)
        self.l1 = self.s.start(self.part(opposite, 1), self.landed(1), self.left)

    def begin_right(self):
        self.r2 = self.s.start(self.part(self.right[self.axis], 1), self.landed(2), self.right)

    def begin_left(self):
        self.l2 = self.s.start(self.part(self.left[self.axis], 0), self.landed(3), self.left)

    def begin(self):
        self.begin_far()
        self.begin_right()
        self.begin_left()

    def middle_right(self):
        self.r1.wait_recv()
        self.landed(0)[...] = self.landed(0)[...] + self.part(self.right[self.axis], 0)[...]
        self.r3 = self.s.start(self.landed(0), self.landed(4), self.right)

    def middle_left(self):
        self.l1.wait_recv()
        self.landed(1)[...] = self.landed(1)[...] + self.part(self.left[self.axis], 1)[...]
        self.l3 = self.s.start(self.landed(1), self.landed(5), self.left)

    def middle(self):
        self.middle_right()
        self.middle_left()

    def end(self):
        me = lax.axis_index(self.axis)
        landed, part = self.landed, self.part
        self.r2.wait_recv()
        self.l2.wait_recv()
        self.r3.wait_recv()
        self.total(0)[...] = (part(me, 0)[...] + landed(3)[...]) + landed(4)[...]
        self.l3.wait_recv()
        self.total(1)[...] = (part(me, 1)[...] + landed(2)[...]) + landed(5)[...]


def whole_kernel(
    enc_src_any,
    enc_hid_any,
    enc_count,
    dec_src_any,
    dec_hid_any,
    dec_count,
    field_any,
    gain_any,
    enc_tiles,
    dec_tiles,
    result_0,
    result_1,
    rms,
    enc_src,
    enc_hid,
    dec_src,
    dec_hid,
    field,
    gain,
    enc_held,
    dec_held,
    table,
    table_s,
    blocks,
    left,
    right,
    sums,
    partial_0,
    partial_1,
    first_in_0,
    first_in_1,
    first_sum_0,
    first_sum_1,
    pair_in_0,
    pair_in_1,
    pair_sum_0,
    pair_sum_1,
    second_in_0,
    second_in_1,
    second_sum_0,
    second_sum_1,
    hidden_0,
    hidden_1,
    back_0,
    back_1,
    core_in_0,
    core_in_1,
    core_sum_0,
    core_sum_1,
    ring_in_0,
    ring_in_1,
    squares,
    square_in,
    local_sems,
    send_sems,
    recv_sems,
):
    partial = (partial_0, partial_1)
    first_in, first_sum = (first_in_0, first_in_1), (first_sum_0, first_sum_1)
    pair_in, pair_sum = (pair_in_0, pair_in_1), (pair_sum_0, pair_sum_1)
    second_in, second_sum = (second_in_0, second_in_1), (second_sum_0, second_sum_1)
    hidden = (hidden_0, hidden_1)
    back, core_in, core_sum = (back_0, back_1), (core_in_0, core_in_1), (core_sum_0, core_sum_1)
    ring_in, result = (ring_in_0, ring_in_1), (result_0, result_1)
    both = (0, 1)
    x, y, z = lax.axis_index(X), lax.axis_index(Y), lax.axis_index(Z)
    zh, core = lax.axis_index(ZH), lax.axis_index(CORE)
    other, twin = 1 - z, 1 - core
    where = {X: x, Y: y}

    lines = [[{axis: shifted(axis, i)} for i in (1, 2, 3)] for axis in (X, Y)]
    stack = [
        {Z: lax.rem(z + dz, 2), ZH: lax.rem(zh + dh, 4), CORE: lax.rem(core + dc, 2)}
        for dz in range(2)
        for dh in range(4)
        for dc in range(2)
        if dz + dh + dc
    ]
    peers = lines[0] + lines[1] + stack
    barrier = pltpu.get_barrier_semaphore()
    small = [
        pltpu.make_async_copy(there, here, local_sems.at[2, i])
        for i, (there, here) in enumerate(
            (
                (enc_src_any, enc_src),
                (enc_hid_any, enc_hid),
                (dec_src_any, dec_src),
                (dec_hid_any, dec_hid),
                (gain_any, gain),
            )
        )
    ]
    field_copy = pltpu.make_async_copy(field_any, field, local_sems.at[2, 7])
    enc_copies = tile_copies(enc_tiles, enc_held, local_sems.at[0])
    dec_copies = tile_copies(dec_tiles, dec_held, local_sems.at[1])
    for copy in (*small, field_copy, *enc_copies):
        copy.start()
    for peer in peers:
        pl.semaphore_signal(barrier, inc=1, device_id=peer, device_id_type=MESH)

    sums[NONE] = jnp.zeros((ROWS, TILE), jnp.float32)
    for copy in small:
        copy.wait()
    before, last = chain(enc_hid[...] & (HID_BLK - 1), enc_count[0])
    before_back, last_back = chain(dec_src[...] & (SRC_BLK - 1), dec_count[0])
    lane = lax.broadcasted_iota(jnp.int32, (CAP, TILE), 1)
    table[...] = jnp.where(
        lane == 0, before, jnp.where(lane == 1, last, jnp.where(lane == 2, before_back, last_back))
    )
    table_copy = pltpu.make_async_copy(table, table_s, local_sems.at[3, 0])
    field_copy.wait()
    for s in range(SRC_BLK):
        value = field[s * ROWS : (s + 1) * ROWS]
        blocks[s] = value
        left[s] = split_pair(value)
        if s == 1:
            table_copy.start()
    for copy in dec_copies:
        copy.start()
    table_copy.wait()
    for chunk, copy in enumerate(enc_copies):
        copy.wait()

        @pl.loop(0, CAP // TILE_DMAS // UNROLL)
        def _(step, chunk=chunk):
            for i in range(UNROLL):
                k = chunk * (CAP // TILE_DMAS) + step * UNROLL + i
                product = full_product(left[enc_src[k] & (SRC_BLK - 1)], stacked_tile(enc_held[k]))
                sums[k] = sums[table_s[k, 0]] + product

    @pl.loop(0, HID_BLK)
    def _(slot):
        for c in both:
            start, rows = CUTS[c]
            partial[c][slot] = sums[table_s[block_in(slot, c), 1], start : start + rows]

    pl.semaphore_wait(barrier, len(peers))
    s = Sender(send_sems, recv_sems)

    order = (2, 1, 3, 0)

    def first_ring(c, i):
        p, q = COLOURS[c]
        there = shifted(q, order[i])
        return RingSum(
            s,
            p,
            lambda m, h: partial[c].at[m * 8 + there * 2 + h],
            lambda n: first_in[c].at[i, n],
            lambda h: first_sum[c].at[there * 2 + h],
        )

    first = [[first_ring(c, i) for i in range(4)] for c in both]
    def part_rows(ref, h, rows):
        return ref.at[pl.ds(h * HALF, rows - HALF if h else HALF)]

    second = [
        RingSum(
            s,
            COLOURS[c][1],
            lambda m, h, c=c: part_rows(pair_sum[c].at[m], h, CUTS[c][1]),
            lambda n, c=c: second_in[c].at[
                n, pl.ds(0, CUTS[c][1] - HALF if n in (1, 2, 5) else HALF)
            ],
            lambda h, c=c: part_rows(second_sum[c], h, CUTS[c][1]),
        )
        for c in both
    ]
    pairs = {}

    def pair_out(c, i):
        there = shifted(COLOURS[c][1], order[i])
        pairs[c, i] = s.start(
            first_sum[c].at[there * 2 + other], pair_in[c].at[there], {Z: other}
        )

    def pair_back(c, i):
        there = shifted(COLOURS[c][1], order[i])
        pairs[c, i].wait_recv()
        pair_sum[c][there] = first_sum[c][there * 2 + z] + pair_in[c][there]

    for i in (0, 1):
        for c in both:
            first[c][i].begin()
    for copy in dec_copies:
        copy.wait()

    @pl.loop(0, CAP)
    def _(k):
        right[k] = stacked_tile(dec_held[k])

    def feed(c, i):
        ring = second[c]
        if i == 0:
            ring.begin_far()
        elif i == 1:
            ring.begin_right()
            ring.middle_right()
        elif i == 2:
            ring.begin_left()
            ring.middle_left()

    for i in range(4):
        for c in both:
            first[c][i].middle()
            if i + 2 < 4:
                first[c][i + 2].begin()
        if i >= 1:
            for c in both:
                first[c][i - 1].end()
                pair_out(c, i - 1)
        if i >= 2:
            for c in both:
                pair_back(c, i - 2)
                feed(c, i - 2)
    for c in both:
        first[c][3].end()
        pair_out(c, 3)
    for c in both:
        pair_back(c, 2)
        feed(c, 2)
    for c in both:
        pair_back(c, 3)
        second[c].end()

    row = lax.broadcasted_iota(jnp.int32, (ROWS, CH), 0)
    column = lax.broadcasted_iota(jnp.int32, (ROWS, CH), 1)
    scale = jnp.sum(
        jnp.where((row >> 1) == column, jnp.broadcast_to(gain[...], (ROWS, CH)), 0.0),
        axis=1,
        keepdims=True,
    )
    values, evens, odds = [], [], []
    for c in both:
        value = second_sum[c][...]
        values.append(value)
        parity = lax.broadcasted_iota(jnp.int32, value.shape, 0) & 1
        square = value * value
        evens.append(jnp.sum(jnp.where(parity == 0, square, 0.0), axis=0, keepdims=True))
        odds.append(jnp.sum(jnp.where(parity == 1, square, 0.0), axis=0, keepdims=True))
    even = lax.rsqrt((evens[0] + evens[1]) * (1.0 / CH) + EPSILON)
    odd = lax.rsqrt((odds[0] + odds[1]) * (1.0 / CH) + EPSILON)
    for c in both:
        start, rows = CUTS[c]
        parity = lax.broadcasted_iota(jnp.int32, (rows, TILE), 0) & 1
        p, q = (where[axis] for axis in COLOURS[c])
        hidden[c][p * 8 + q * 2 + z] = (
            values[c] * scale[start : start + rows] * jnp.where(parity == 0, even, odd)
        )

    def outer_block(c, m, step, far):
        there = shifted(COLOURS[c][1], step)
        return hidden[c].at[m * 8 + there * 2 + (other if far else z)]

    def inner_block(c, step):
        p, q = COLOURS[c]
        return hidden[c].at[where[p] * 8 + shifted(q, step) * 2 + z]

    def send(block, axis, step):
        return s.start(block, block, {axis: shifted(axis, step)})

    inner, paired, outer, passed = {}, {}, {}, {}

    def to_pair(c, step):
        paired[c, step] = send(inner_block(c, step), Z, 1)

    def to_line(c, step, far):
        p = COLOURS[c][0]
        block = outer_block(c, where[p], step, far)
        outer[c, step, far] = [send(block, p, 1), send(block, p, -1)]

    def along_line(c, step, far):
        p = COLOURS[c][0]
        from_left, from_right = outer[c, step, far]
        if far:
            from_right.wait_recv()
            passed[c, step, far] = send(outer_block(c, shifted(p, 1), step, far), p, -1)
        else:
            from_left.wait_recv()
            passed[c, step, far] = send(outer_block(c, shifted(p, -1), step, far), p, 1)

    def settle_line(c, step, far):
        outer[c, step, far][0 if far else 1].wait_recv()
        passed[c, step, far].wait_recv()

    for c in both:
        q, mine = COLOURS[c][1], inner_block(c, 0)
        inner[c] = [send(mine, q, 1), send(mine, q, -1)]
        to_pair(c, 0)
    for c in both:
        to_line(c, 0, False)
    for c in both:
        q, rows = COLOURS[c][1], CUTS[c][1]
        from_left, from_right = inner[c]
        from_left.wait_recv()
        inner[c] = [send(part_rows(inner_block(c, -1), 0, rows), q, 1)]
        to_pair(c, -1)
        from_right.wait_recv()
        inner[c].append(send(part_rows(inner_block(c, 1), 1, rows), q, -1))
        to_pair(c, 1)
        to_line(c, -1, False)
        to_line(c, 1, False)
    for c in both:
        paired[c, 0].wait_recv()
        to_line(c, 0, True)
    for c in both:
        along_line(c, 0, False)
    for c in both:
        for copy in inner[c]:
            copy.wait_recv()
        to_pair(c, 2)
        to_line(c, 2, False)
    for c in both:
        for step in (-1, 1):
            paired[c, step].wait_recv()
            to_line(c, step, True)
    for c in both:
        along_line(c, -1, False)
        along_line(c, 1, False)
        along_line(c, 0, True)
    for c in both:
        paired[c, 2].wait_recv()
        to_line(c, 2, True)
    for c in both:
        along_line(c, 2, False)
        along_line(c, -1, True)
        along_line(c, 1, True)
    for c in both:
        along_line(c, 2, True)
    for key in passed:
        settle_line(*key)

    @pl.loop(0, CAP // UNROLL)
    def _(step):
        for i in range(UNROLL):
            k = step * UNROLL + i
            block = dec_hid[k] & (HID_BLK - 1)
            pieces = [split_pair(hidden[c][slot_of(block, c)]) for c in both]
            product = full_product(jnp.concatenate(pieces, axis=0), right[k])
            sums[k] = sums[table_s[k, 2]] + product

    @pl.loop(0, SRC_BLK)
    def _(i):
        for c in both:
            start, rows = CUTS[c]
            back[c][i] = sums[table_s[i, 3], start : start + rows]

    crossing = {}
    for step in order:
        m = lax.rem(zh + step, 4)
        for c in both:
            crossing[step, c] = s.start(
                back[c].at[twin * 4 + m], core_in[c].at[m], {CORE: twin}
            )
    column_ring = RingSum(
        s,
        ZH,
        lambda m, h: core_sum[h].at[m],
        lambda n: ring_in[(0, 1, 1, 0, 0, 1)[n]].at[(0, 0, 1, 1, 2, 2)[n]],
        lambda h: result[h].at[core * 4 + zh],
    )
    for step in order:
        m = lax.rem(zh + step, 4)
        for c in both:
            crossing[step, c].wait_recv()
            core_sum[c][m] = back[c][core * 4 + m] + core_in[c][m]
        if step == 2:
            column_ring.begin_far()
        elif step == 1:
            column_ring.begin_right()
        elif step == 3:
            column_ring.begin_left()
    column_ring.middle()
    column_ring.end()

    def own_half(step, h):
        return result[h].at[core * 4 + lax.rem(zh + step, 4)]

    to_right = [send(own_half(0, 0), ZH, 1)]
    to_left = [send(own_half(0, 1), ZH, -1)]
    to_right.append(send(own_half(0, 1), ZH, 1))
    to_left.append(send(own_half(0, 0), ZH, -1))
    total = None
    for c in both:
        start, rows = CUTS[c]
        error = result[c][core * 4 + zh] - blocks[core * 4 + zh, start : start + rows]
        by_row = jnp.sum(error * error, axis=1, keepdims=True)
        row = start + lax.broadcasted_iota(jnp.int32, (rows, TILE), 0)
        column = lax.broadcasted_iota(jnp.int32, (rows, TILE), 1)
        part = jnp.sum(jnp.where((row >> 1) == column, by_row, 0.0), axis=0, keepdims=True)
        total = part if total is None else total + part
    squares[0] = jnp.broadcast_to(total, (8, TILE))

    def to_twin(step, c):
        block = own_half(step, c)
        return s.start(block, block, {CORE: twin})

    twins = [to_twin(0, c) for c in both]

    def exchange(stage, first_slot, those):
        return [
            s.start(squares.at[stage], square_in.at[first_slot + i], peer)
            for i, peer in enumerate(those)
        ]

    def collect(stage, first_slot, copies):
        value = squares[stage]
        for i, copy in enumerate(copies):
            copy.wait_recv()
            value = value + square_in[first_slot + i]
        squares[stage + 1] = value

    copies = exchange(0, 0, lines[0])
    collect(0, 0, copies)
    copies = exchange(1, 3, lines[1])
    to_right[0].wait_recv()
    passing = [send(own_half(3, 0), ZH, 1)]
    to_left[0].wait_recv()
    passing.append(send(own_half(1, 1), ZH, -1))
    twins += [to_twin(3, 0), to_twin(1, 1)]
    collect(1, 3, copies)
    copies = exchange(2, 6, stack)
    to_right[1].wait_recv()
    to_left[1].wait_recv()
    twins += [to_twin(3, 1), to_twin(1, 0)]
    for c in both:
        passing[c].wait_recv()
        twins.append(to_twin(2, c))
    collect(2, 6, copies)
    rms[...] = jnp.sqrt(squares[3] * (1.0 / TOTAL_POINTS) + EPSILON)
    for copy in twins:
        copy.wait_recv()
    s.finish()


def assemble_kernel(result_0, result_1, rms, out, rms_out):
    for i in range(SRC_BLK):
        for (start, rows), part in zip(CUTS, (result_0, result_1)):
            out[i * ROWS + start : i * ROWS + start + rows] = part[i]
    rms_out[...] = rms[0:1, 0:CH]


VMEM = pl.BlockSpec(memory_space=pltpu.VMEM)
HBM = pl.BlockSpec(memory_space=pltpu.HBM)
SMEM = pl.BlockSpec(memory_space=pltpu.SMEM)


def coloured(*lead):
    return [pltpu.VMEM((*lead, rows, TILE), jnp.float32) for _, rows in CUTS]


def body(
    source_field,
    hidden_gain,
    enc_tiles,
    enc_src_block,
    enc_hid_block,
    enc_count,
    dec_tiles,
    dec_src_block,
    dec_hid_block,
    dec_count,
):
    rows = source_field.transpose(0, 2, 1, 3).reshape(SRC_BLK * ROWS, TILE)
    held = pltpu.VMEM((CAP, TILE, TILE), jnp.float32)
    pieces = pl.pallas_call(
        whole_kernel,
        out_shape=(*coloured(SRC_BLK), pltpu.VMEM((8, TILE), jnp.float32)),
        in_specs=[HBM, HBM, SMEM, HBM, HBM, SMEM, HBM, HBM, HBM, HBM],
        out_specs=(VMEM, VMEM, VMEM),
        scratch_shapes=[
            pltpu.SMEM((CAP,), jnp.int32),
            pltpu.VMEM((1, CAP), jnp.int32),
            pltpu.VMEM((1, CAP), jnp.int32),
            pltpu.SMEM((CAP,), jnp.int32),
            pltpu.VMEM((SRC_BLK * ROWS, TILE), jnp.float32),
            pltpu.VMEM((1, CH), jnp.float32),
            held,
            held,
            pltpu.VMEM((CAP, TILE), jnp.int32),
            pltpu.SMEM((CAP, TILE), jnp.int32),
            pltpu.VMEM((SRC_BLK, ROWS, TILE), jnp.float32),
            pltpu.VMEM((SRC_BLK, ROWS, 2 * TILE), jnp.bfloat16),
            pltpu.VMEM((CAP, 2 * TILE, 2 * TILE), jnp.bfloat16),
            pltpu.VMEM((CAP + 1, ROWS, TILE), jnp.float32),
            *coloured(HID_BLK),
            *coloured(4, 6),
            *coloured(8),
            *coloured(4),
            *coloured(4),
            *[pltpu.VMEM((6, 56, TILE), jnp.float32)] * 2,
            *coloured(),
            *coloured(HID_BLK),
            *coloured(SRC_BLK),
            *coloured(4),
            *coloured(4),
            *coloured(3),
            pltpu.VMEM((4, 8, TILE), jnp.float32),
            pltpu.VMEM((21, 8, TILE), jnp.float32),
            pltpu.SemaphoreType.DMA((4, 8)),
            pltpu.SemaphoreType.DMA((N_SEMS,)),
            pltpu.SemaphoreType.DMA((N_SEMS,)),
        ],
        compiler_params=pltpu.CompilerParams(collective_id=0, has_side_effects=True),
    )(
        enc_src_block,
        enc_hid_block.reshape(1, CAP),
        enc_count,
        dec_src_block.reshape(1, CAP),
        dec_hid_block,
        dec_count,
        rows,
        hidden_gain.reshape(1, CH),
        enc_tiles,
        dec_tiles,
    )
    returned, rms = pl.pallas_call(
        assemble_kernel,
        out_shape=(
            jax.ShapeDtypeStruct((SRC_BLK * ROWS, TILE), jnp.float32),
            jax.ShapeDtypeStruct((1, CH), jnp.float32),
        ),
        in_specs=[VMEM] * 3,
        out_specs=(VMEM, VMEM),
    )(*[pltpu.with_memory_space_constraint(piece, pltpu.VMEM) for piece in pieces])
    returned = returned.reshape(SRC_BLK, CH, BATCH, TILE).transpose(0, 2, 1, 3)
    return returned, rms.reshape(CH)


def solution(mesh):
    split = Mesh(mesh.devices.reshape(4, 2, 4, 4, 2), AXES)
    every = P(AXES)
    in_specs = (
        P(SRC, None, None, None),
        P(),
        P(AXES, None, None),
        every,
        every,
        every,
        P(AXES, None, None),
        every,
        every,
        every,
    )
    out_specs = (P(SRC, None, None, None), P())
    return jax.shard_map(body, mesh=split, in_specs=in_specs, out_specs=out_specs, check_vma=False)
```

```python
import jax
import jax.numpy as jnp
from jax import lax
from jax.experimental import pallas as pl
from jax.experimental.pallas import tpu as pltpu
from jax.sharding import Mesh
from jax.sharding import PartitionSpec as P

CH = 98
BATCH = 2
TILE = 128
ROWS = CH * BATCH
SRC_BLK = 8
HID_BLK = 32
CAP = 32
NONE = CAP
TOTAL_POINTS = 256 * BATCH * TILE
EPSILON = 1e-06
AXES = ("src_0", "src_1", "src_2", "hid_0", "hid_1")
SRC = ("src_0", "src_1", "src_2")
SIZES = {"src_0": 4, "src_1": 2, "src_2": 4, "hid_0": 4, "hid_1": 2}
MESH = pl.DeviceIdType.MESH
TILE_DMAS = 4
UNROLL = 4
N_SEMS = 341

X, Z, Y, ZH, CORE = AXES
STEP = 112
CUTS = ((0, 48), (48, 50))
HALF = 24
COLOURS = ((X, Y), (Y, X))
BOTH = (0, 1)
ORDER = (2, 1, 3, 0)


def slot_of(block, colour):
    x, z, y = block >> 3, (block >> 2) & 1, block & 3
    if colour == 0:
        return x * 8 + y * 2 + z
    return y * 8 + x * 2 + z


def block_in(slot, colour):
    p, q, z = slot >> 3, (slot >> 1) & 3, slot & 1
    if colour == 0:
        return p * 8 + z * 4 + q
    return q * 8 + z * 4 + p


def split_pair(value):
    high = value.astype(jnp.bfloat16)
    low = (value - high.astype(jnp.float32)).astype(jnp.bfloat16)
    return jnp.concatenate([high, low], axis=1)


def stacked_tile(tile):
    row = split_pair(tile)
    return jnp.concatenate([row, row], axis=0)


def full_product(left, right):
    both = jnp.dot(left, right, preferred_element_type=jnp.float32)
    return both[:, :TILE] + both[:, TILE:]


def tile_copies(tiles, held, sems):
    part = CAP // TILE_DMAS
    return [
        pltpu.make_async_copy(
            tiles.at[pl.ds(i * part, part)], held.at[pl.ds(i * part, part)], sems.at[i]
        )
        for i in range(TILE_DMAS)
    ]


def shifted(axis, step):
    size = SIZES[axis]
    return lax.rem(lax.axis_index(axis) + (step + size), size)


def chain(targets, count):
    row = lax.broadcasted_iota(jnp.int32, (CAP, CAP), 0)
    lane = lax.broadcasted_iota(jnp.int32, (CAP, CAP), 1)
    along = jnp.broadcast_to(targets, (CAP, CAP))
    down = jnp.sum(jnp.where(row == lane, along, 0), axis=1, keepdims=True)
    live = lane < count
    before = jnp.max(jnp.where(live & (lane < row) & (along == down), lane, -1), axis=1, keepdims=True)
    last = jnp.max(jnp.where(live & (along == row), lane, -1), axis=1, keepdims=True)
    return jnp.where(before < 0, NONE, before), jnp.where(last < 0, NONE, last)


class Sender:
    def __init__(self, send_sems, recv_sems):
        self.send_sems, self.recv_sems, self.count, self.sent = send_sems, recv_sems, 0, []

    def start(self, src, dst, where):
        i = self.count
        self.count += 1
        copy = pltpu.make_async_remote_copy(
            src_ref=src,
            dst_ref=dst,
            send_sem=self.send_sems.at[i],
            recv_sem=self.recv_sems.at[i],
            device_id=where,
            device_id_type=MESH,
        )
        copy.start()
        self.sent.append(copy)
        return copy

    def along(self, block, axis, step):
        return self.start(block, block, {axis: shifted(axis, step)})

    def finish(self):
        for copy in self.sent:
            copy.wait_send()


class RingSum:
    def __init__(self, sender, axis, part, landed, total):
        self.s, self.axis, self.part, self.landed, self.total = sender, axis, part, landed, total
        self.right, self.left = {axis: shifted(axis, 1)}, {axis: shifted(axis, -1)}

    def begin_far(self):
        opposite = shifted(self.axis, 2)
        self.r1 = self.s.start(self.part(opposite, 0), self.landed(0), self.right)
        self.l1 = self.s.start(self.part(opposite, 1), self.landed(1), self.left)

    def begin_right(self):
        self.r2 = self.s.start(self.part(self.right[self.axis], 1), self.landed(2), self.right)

    def begin_left(self):
        self.l2 = self.s.start(self.part(self.left[self.axis], 0), self.landed(3), self.left)

    def begin(self):
        self.begin_far()
        self.begin_right()
        self.begin_left()

    def middle_right(self):
        self.r1.wait_recv()
        self.landed(0)[...] = self.landed(0)[...] + self.part(self.right[self.axis], 0)[...]
        self.r3 = self.s.start(self.landed(0), self.landed(4), self.right)

    def middle_left(self):
        self.l1.wait_recv()
        self.landed(1)[...] = self.landed(1)[...] + self.part(self.left[self.axis], 1)[...]
        self.l3 = self.s.start(self.landed(1), self.landed(5), self.left)

    def middle(self):
        self.middle_right()
        self.middle_left()

    def end(self):
        me = lax.axis_index(self.axis)
        landed, part = self.landed, self.part
        self.r2.wait_recv()
        self.l2.wait_recv()
        self.r3.wait_recv()
        self.total(0)[...] = (part(me, 0)[...] + landed(3)[...]) + landed(4)[...]
        self.l3.wait_recv()
        self.total(1)[...] = (part(me, 1)[...] + landed(2)[...]) + landed(5)[...]


def part_rows(ref, h, rows):
    return ref.at[pl.ds(h * HALF, rows - HALF if h else HALF)]


def whole_kernel(
    enc_src_any,
    enc_hid_any,
    enc_count,
    dec_src_any,
    dec_hid_any,
    dec_count,
    field_any,
    gain_any,
    enc_tiles,
    dec_tiles,
    result_00,
    result_01,
    result_10,
    result_11,
    rms,
    enc_src,
    enc_hid,
    dec_src,
    dec_hid,
    field,
    gain,
    enc_held,
    dec_held,
    table,
    table_s,
    blocks,
    left,
    right,
    sums,
    partial,
    first_in,
    first_sum,
    pair_in,
    pair_sum,
    second_in,
    second_sum,
    hidden,
    back,
    core_in,
    core_sum,
    ring_in,
    squares,
    square_in,
    local_sems,
    send_sems,
    recv_sems,
):
    result = ((result_00, result_01), (result_10, result_11))
    x, y, z = lax.axis_index(X), lax.axis_index(Y), lax.axis_index(Z)
    zh, core = lax.axis_index(ZH), lax.axis_index(CORE)
    other, twin = 1 - z, 1 - core
    where = {X: x, Y: y}

    lines = [[{axis: shifted(axis, i)} for i in (1, 2, 3)] for axis in (X, Y)]
    stack = [
        {Z: lax.rem(z + dz, 2), ZH: lax.rem(zh + dh, 4), CORE: lax.rem(core + dc, 2)}
        for dz in range(2)
        for dh in range(4)
        for dc in range(2)
        if dz + dh + dc
    ]
    peers = lines[0] + lines[1] + stack
    barrier = pltpu.get_barrier_semaphore()
    small = [
        pltpu.make_async_copy(there, here, local_sems.at[2, i])
        for i, (there, here) in enumerate(
            (
                (enc_src_any, enc_src),
                (enc_hid_any, enc_hid),
                (dec_src_any, dec_src),
                (dec_hid_any, dec_hid),
                (gain_any, gain),
            )
        )
    ]
    field_copy = pltpu.make_async_copy(field_any, field, local_sems.at[2, 7])
    enc_copies = tile_copies(enc_tiles, enc_held, local_sems.at[0])
    dec_copies = tile_copies(dec_tiles, dec_held, local_sems.at[1])
    for copy in (*small, field_copy, *enc_copies):
        copy.start()
    for peer in peers:
        pl.semaphore_signal(barrier, inc=1, device_id=peer, device_id_type=MESH)

    sums[NONE] = jnp.zeros((STEP + CH, TILE), jnp.float32)
    for copy in small:
        copy.wait()
    before, last = chain(enc_hid[...] & (HID_BLK - 1), enc_count[0])
    before_back, last_back = chain(dec_src[...] & (SRC_BLK - 1), dec_count[0])
    lane = lax.broadcasted_iota(jnp.int32, (CAP, TILE), 1)
    table[...] = jnp.where(
        lane == 0, before, jnp.where(lane == 1, last, jnp.where(lane == 2, before_back, last_back))
    )
    table_copy = pltpu.make_async_copy(table, table_s, local_sems.at[3, 0])
    field_copy.wait()
    for i in range(SRC_BLK):
        left[i, CH:STEP] = jnp.zeros((STEP - CH, 2 * TILE), jnp.bfloat16)
        for b in BOTH:
            value = field[pl.ds(i * ROWS + b, CH, stride=2)]
            blocks[b, i] = value
            left[i, b * STEP : b * STEP + CH] = split_pair(value)
        if i == 1:
            table_copy.start()
    for copy in dec_copies:
        copy.start()
    table_copy.wait()
    for chunk, copy in enumerate(enc_copies):
        copy.wait()

        @pl.loop(0, CAP // TILE_DMAS // UNROLL)
        def _(step, chunk=chunk):
            for i in range(UNROLL):
                k = chunk * (CAP // TILE_DMAS) + step * UNROLL + i
                product = full_product(left[enc_src[k] & (SRC_BLK - 1)], stacked_tile(enc_held[k]))
                sums[k] = sums[table_s[k, 0]] + product

    @pl.loop(0, HID_BLK)
    def _(slot):
        for c in BOTH:
            start, rows = CUTS[c]
            k = table_s[block_in(slot, c), 1]
            for b in BOTH:
                partial[b][c][slot] = sums[k, b * STEP + start : b * STEP + start + rows]

    pl.semaphore_wait(barrier, len(peers))
    s = Sender(send_sems, recv_sems)
    identity = lax.broadcasted_iota(jnp.int32, (CH, CH), 0) == lax.broadcasted_iota(
        jnp.int32, (CH, CH), 1
    )
    scale = jnp.sum(
        jnp.where(identity, jnp.broadcast_to(gain[...], (CH, CH)), 0.0), axis=1, keepdims=True
    )

    def reduce_steps(b):
        def first_ring(c, i):
            p, q = COLOURS[c]
            there = shifted(q, ORDER[i])
            return RingSum(
                s,
                p,
                lambda m, h: partial[b][c].at[m * 8 + there * 2 + h],
                lambda n: first_in[b][c].at[i, n],
                lambda h: first_sum[b][c].at[there * 2 + h],
            )

        def second_ring(c):
            rows = CUTS[c][1]
            return RingSum(
                s,
                COLOURS[c][1],
                lambda m, h: part_rows(pair_sum[b][c].at[m], h, rows),
                lambda n: second_in[b][c].at[n, pl.ds(0, rows - HALF if n in (1, 2, 5) else HALF)],
                lambda h: part_rows(second_sum[b][c], h, rows),
            )

        first = [[first_ring(c, i) for i in range(4)] for c in BOTH]
        second = [second_ring(c) for c in BOTH]
        pairs = {}

        def settle(i):
            for c in BOTH:
                first[c][i].end()
                there = shifted(COLOURS[c][1], ORDER[i])
                pairs[c, i] = s.start(
                    first_sum[b][c].at[there * 2 + other], pair_in[b][c].at[there], {Z: other}
                )

        def pair_back(c, i):
            there = shifted(COLOURS[c][1], ORDER[i])
            pairs[c, i].wait_recv()
            pair_sum[b][c][there] = first_sum[b][c][there * 2 + z] + pair_in[b][c][there]

        for i in (0, 1):
            for c in BOTH:
                first[c][i].begin()
        yield
        for c in BOTH:
            first[c][0].middle()
            first[c][2].begin()
        yield
        for c in BOTH:
            first[c][1].middle()
            first[c][3].begin()
        settle(0)
        yield
        for c in BOTH:
            first[c][2].middle()
        settle(1)
        for c in BOTH:
            pair_back(c, 0)
            second[c].begin_far()
        yield
        for c in BOTH:
            first[c][3].middle()
        settle(2)
        for c in BOTH:
            pair_back(c, 1)
            second[c].begin_right()
            second[c].middle_right()
        yield
        settle(3)
        for c in BOTH:
            pair_back(c, 2)
            second[c].begin_left()
            second[c].middle_left()
        yield
        squares_sum = None
        for c in BOTH:
            pair_back(c, 3)
            second[c].end()
            value = second_sum[b][c][...]
            square = jnp.sum(value * value, axis=0, keepdims=True)
            squares_sum = square if squares_sum is None else squares_sum + square
        factor = lax.rsqrt(squares_sum * (1.0 / CH) + EPSILON)
        for c in BOTH:
            start, rows = CUTS[c]
            p, q = (where[axis] for axis in COLOURS[c])
            hidden[b][c][p * 8 + q * 2 + z] = (
                second_sum[b][c][...] * scale[start : start + rows] * factor
            )

    def gather_steps(b):
        inner, paired, outer, passed = {}, {}, {}, {}

        def outer_block(c, m, step, far):
            there = shifted(COLOURS[c][1], step)
            return hidden[b][c].at[m * 8 + there * 2 + (other if far else z)]

        def inner_block(c, step):
            p, q = COLOURS[c]
            return hidden[b][c].at[where[p] * 8 + shifted(q, step) * 2 + z]

        def to_pair(c, step):
            paired[c, step] = s.along(inner_block(c, step), Z, 1)

        def to_line(c, step, far):
            p = COLOURS[c][0]
            block = outer_block(c, where[p], step, far)
            outer[c, step, far] = [s.along(block, p, 1), s.along(block, p, -1)]

        def along_line(c, step, far):
            p = COLOURS[c][0]
            from_left, from_right = outer[c, step, far]
            if far:
                from_right.wait_recv()
                passed[c, step, far] = s.along(outer_block(c, shifted(p, 1), step, far), p, -1)
            else:
                from_left.wait_recv()
                passed[c, step, far] = s.along(outer_block(c, shifted(p, -1), step, far), p, 1)

        for c in BOTH:
            q, mine = COLOURS[c][1], inner_block(c, 0)
            inner[c] = [s.along(mine, q, 1), s.along(mine, q, -1)]
            to_pair(c, 0)
        for c in BOTH:
            to_line(c, 0, False)
        yield
        for c in BOTH:
            q, rows = COLOURS[c][1], CUTS[c][1]
            from_left, from_right = inner[c]
            from_left.wait_recv()
            inner[c] = [s.along(part_rows(inner_block(c, -1), 0, rows), q, 1)]
            to_pair(c, -1)
            from_right.wait_recv()
            inner[c].append(s.along(part_rows(inner_block(c, 1), 1, rows), q, -1))
            to_pair(c, 1)
            to_line(c, -1, False)
            to_line(c, 1, False)
        yield
        for c in BOTH:
            paired[c, 0].wait_recv()
            to_line(c, 0, True)
        for c in BOTH:
            along_line(c, 0, False)
        yield
        for c in BOTH:
            for copy in inner[c]:
                copy.wait_recv()
            to_pair(c, 2)
            to_line(c, 2, False)
        yield
        for c in BOTH:
            for step in (-1, 1):
                paired[c, step].wait_recv()
                to_line(c, step, True)
        for c in BOTH:
            along_line(c, -1, False)
            along_line(c, 1, False)
            along_line(c, 0, True)
        yield
        for c in BOTH:
            paired[c, 2].wait_recv()
            to_line(c, 2, True)
        for c in BOTH:
            along_line(c, 2, False)
            along_line(c, -1, True)
            along_line(c, 1, True)
        yield
        for c in BOTH:
            along_line(c, 2, True)
        yield
        for c, step, far in passed:
            outer[c, step, far][0 if far else 1].wait_recv()
            passed[c, step, far].wait_recv()

    def decode(b):
        @pl.loop(0, CAP // UNROLL)
        def _(step):
            for i in range(UNROLL):
                k = step * UNROLL + i
                block = dec_hid[k] & (HID_BLK - 1)
                pieces = [split_pair(hidden[b][c][slot_of(block, c)]) for c in BOTH]
                product = full_product(jnp.concatenate(pieces, axis=0), right[k])
                here = slice(b * STEP, b * STEP + CH)
                sums[k, here] = sums[table_s[k, 2], here] + product

        @pl.loop(0, SRC_BLK)
        def _(i):
            k = table_s[i, 3]
            for c in BOTH:
                start, rows = CUTS[c]
                back[b][c][i] = sums[k, b * STEP + start : b * STEP + start + rows]

    def column_steps(b):
        crossing = {}
        for step in ORDER:
            m = lax.rem(zh + step, 4)
            for c in BOTH:
                crossing[step, c] = s.start(
                    back[b][c].at[twin * 4 + m], core_in[b][c].at[m], {CORE: twin}
                )
        yield
        ring = RingSum(
            s,
            ZH,
            lambda m, h: core_sum[b][h].at[m],
            lambda n: ring_in[b][(0, 1, 1, 0, 0, 1)[n]].at[(0, 0, 1, 1, 2, 2)[n]],
            lambda h: result[b][h].at[core * 4 + zh],
        )
        for step in ORDER:
            m = lax.rem(zh + step, 4)
            for c in BOTH:
                crossing[step, c].wait_recv()
                core_sum[b][c][m] = back[b][c][core * 4 + m] + core_in[b][c][m]
            if step == 2:
                ring.begin_far()
            elif step == 1:
                ring.begin_right()
            elif step == 3:
                ring.begin_left()
        yield
        ring.middle()
        yield
        ring.end()

        def own_half(step, h):
            return result[b][h].at[core * 4 + lax.rem(zh + step, 4)]

        def to_twin(step, c):
            return s.along(own_half(step, c), CORE, 1)

        to_right = [s.along(own_half(0, 0), ZH, 1)]
        to_left = [s.along(own_half(0, 1), ZH, -1)]
        to_right.append(s.along(own_half(0, 1), ZH, 1))
        to_left.append(s.along(own_half(0, 0), ZH, -1))
        twins = [to_twin(0, c) for c in BOTH]
        yield
        to_right[0].wait_recv()
        passing = [s.along(own_half(3, 0), ZH, 1)]
        to_left[0].wait_recv()
        passing.append(s.along(own_half(1, 1), ZH, -1))
        twins += [to_twin(3, 0), to_twin(1, 1)]
        yield
        to_right[1].wait_recv()
        to_left[1].wait_recv()
        twins += [to_twin(3, 1), to_twin(1, 0)]
        for c in BOTH:
            passing[c].wait_recv()
            twins.append(to_twin(2, c))
        yield
        for copy in twins:
            copy.wait_recv()

    def own_squares(b):
        line = None
        for c in BOTH:
            start, rows = CUTS[c]
            error = result[b][c][core * 4 + zh] - blocks[b, core * 4 + zh, start : start + rows]
            by_row = jnp.sum(error * error, axis=1, keepdims=True)
            row = start + lax.broadcasted_iota(jnp.int32, (rows, TILE), 0)
            column = lax.broadcasted_iota(jnp.int32, (rows, TILE), 1)
            part = jnp.sum(jnp.where(row == column, by_row, 0.0), axis=0, keepdims=True)
            line = part if line is None else line + part
        return jnp.broadcast_to(line, (8, TILE))

    def exchange(stage, first_slot, those):
        return [
            s.start(squares.at[stage], square_in.at[first_slot + i], peer)
            for i, peer in enumerate(those)
        ]

    def collect(stage, first_slot, copies):
        value = squares[stage]
        for i, copy in enumerate(copies):
            copy.wait_recv()
            value = value + square_in[first_slot + i]
        squares[stage + 1] = value

    reduces = [reduce_steps(b) for b in BOTH]
    gathers = [gather_steps(b) for b in BOTH]
    columns = [column_steps(b) for b in BOTH]

    def go(*those):
        for steps in those:
            next(steps, None)

    r0, r1 = reduces
    g0, g1 = gathers
    z0, z1 = columns
    go(r0)
    for copy in dec_copies:
        copy.wait()

    @pl.loop(0, CAP)
    def _(k):
        right[k] = stacked_tile(dec_held[k])

    go(r0, r0, r0, r0, r1, r0, r1, r0, g0, r1, g0, r1, g0, r1, g0, r1, g0, r1, g1)
    go(g0, g1, g0, g1, g0)
    decode(0)
    go(z0, g1, z0, g1, z0, g1, z0, g1, z0, g1)
    go(z0)
    decode(1)
    go(z1, z1, z0, z1, z0, z1)
    squares[0] = own_squares(0) + own_squares(1)
    copies = exchange(0, 0, lines[0])
    collect(0, 0, copies)
    copies = exchange(1, 3, lines[1])
    go(z1)
    collect(1, 3, copies)
    copies = exchange(2, 6, stack)
    go(z1)
    collect(2, 6, copies)
    rms[...] = jnp.sqrt(squares[3] * (1.0 / TOTAL_POINTS) + EPSILON)
    go(z1)
    for steps in (*reduces, *gathers, *columns):
        for _ in steps:
            raise ValueError("steps left")
    assert s.count == N_SEMS
    s.finish()


def assemble_kernel(result_00, result_01, result_10, result_11, rms, out, rms_out):
    result = ((result_00, result_01), (result_10, result_11))
    for i in range(SRC_BLK):
        for b in BOTH:
            for c in BOTH:
                start, rows = CUTS[c]
                out[pl.ds(i * ROWS + start * 2 + b, rows, stride=2)] = result[b][c][i]
    rms_out[...] = rms[0:1, 0:CH]


VMEM = pl.BlockSpec(memory_space=pltpu.VMEM)
HBM = pl.BlockSpec(memory_space=pltpu.HBM)
SMEM = pl.BlockSpec(memory_space=pltpu.SMEM)


def coloured(*lead):
    return [pltpu.VMEM((*lead, rows, TILE), jnp.float32) for _, rows in CUTS]


def pieces(*lead):
    return [coloured(*lead) for _ in BOTH]


def body(
    source_field,
    hidden_gain,
    enc_tiles,
    enc_src_block,
    enc_hid_block,
    enc_count,
    dec_tiles,
    dec_src_block,
    dec_hid_block,
    dec_count,
):
    rows = source_field.transpose(0, 2, 1, 3).reshape(SRC_BLK * ROWS, TILE)
    held = pltpu.VMEM((CAP, TILE, TILE), jnp.float32)
    parts = pl.pallas_call(
        whole_kernel,
        out_shape=(
            *coloured(SRC_BLK),
            *coloured(SRC_BLK),
            pltpu.VMEM((8, TILE), jnp.float32),
        ),
        in_specs=[HBM, HBM, SMEM, HBM, HBM, SMEM, HBM, HBM, HBM, HBM],
        out_specs=(VMEM,) * 5,
        scratch_shapes=[
            pltpu.SMEM((CAP,), jnp.int32),
            pltpu.VMEM((1, CAP), jnp.int32),
            pltpu.VMEM((1, CAP), jnp.int32),
            pltpu.SMEM((CAP,), jnp.int32),
            pltpu.VMEM((SRC_BLK * ROWS, TILE), jnp.float32),
            pltpu.VMEM((1, CH), jnp.float32),
            held,
            held,
            pltpu.VMEM((CAP, TILE), jnp.int32),
            pltpu.SMEM((CAP, TILE), jnp.int32),
            pltpu.VMEM((BATCH, SRC_BLK, CH, TILE), jnp.float32),
            pltpu.VMEM((SRC_BLK, STEP + CH, 2 * TILE), jnp.bfloat16),
            pltpu.VMEM((CAP, 2 * TILE, 2 * TILE), jnp.bfloat16),
            pltpu.VMEM((CAP + 1, STEP + CH, TILE), jnp.float32),
            pieces(HID_BLK),
            pieces(4, 6),
            pieces(8),
            pieces(4),
            pieces(4),
            [[pltpu.VMEM((6, 32, TILE), jnp.float32)] * 2] * 2,
            pieces(),
            pieces(HID_BLK),
            pieces(SRC_BLK),
            pieces(4),
            pieces(4),
            pieces(3),
            pltpu.VMEM((4, 8, TILE), jnp.float32),
            pltpu.VMEM((21, 8, TILE), jnp.float32),
            pltpu.SemaphoreType.DMA((4, 8)),
            pltpu.SemaphoreType.DMA((N_SEMS,)),
            pltpu.SemaphoreType.DMA((N_SEMS,)),
        ],
        compiler_params=pltpu.CompilerParams(collective_id=0, has_side_effects=True),
    )(
        enc_src_block,
        enc_hid_block.reshape(1, CAP),
        enc_count,
        dec_src_block.reshape(1, CAP),
        dec_hid_block,
        dec_count,
        rows,
        hidden_gain.reshape(1, CH),
        enc_tiles,
        dec_tiles,
    )
    returned, rms = pl.pallas_call(
        assemble_kernel,
        out_shape=(
            jax.ShapeDtypeStruct((SRC_BLK * ROWS, TILE), jnp.float32),
            jax.ShapeDtypeStruct((1, CH), jnp.float32),
        ),
        in_specs=[VMEM] * 5,
        out_specs=(VMEM, VMEM),
    )(*[pltpu.with_memory_space_constraint(part, pltpu.VMEM) for part in parts])
    returned = returned.reshape(SRC_BLK, CH, BATCH, TILE).transpose(0, 2, 1, 3)
    return returned, rms.reshape(CH)


def solution(mesh):
    split = Mesh(mesh.devices.reshape(4, 2, 4, 4, 2), AXES)
    every = P(AXES)
    in_specs = (
        P(SRC, None, None, None),
        P(),
        P(AXES, None, None),
        every,
        every,
        every,
        P(AXES, None, None),
        every,
        every,
        every,
    )
    out_specs = (P(SRC, None, None, None), P())
    return jax.shard_map(body, mesh=split, in_specs=in_specs, out_specs=out_specs, check_vma=False)
```

```python
import jax
import jax.numpy as jnp
from jax import lax
from jax.experimental import pallas as pl
from jax.experimental.pallas import tpu as pltpu
from jax.sharding import Mesh
from jax.sharding import PartitionSpec as P

CH = 98
BATCH = 2
TILE = 128
ROWS = CH * BATCH
SRC_BLK = 8
HID_BLK = 32
CAP = 32
NONE = CAP
TOTAL_POINTS = 256 * BATCH * TILE
EPSILON = 1e-06
AXES = ("src_0", "src_1", "src_2", "hid_0", "hid_1")
SRC = ("src_0", "src_1", "src_2")
SIZES = {"src_0": 4, "src_1": 2, "src_2": 4, "hid_0": 4, "hid_1": 2}
MESH = pl.DeviceIdType.MESH
TILE_DMAS = 4
UNROLL = 4
N_SEMS = 200

X, Z, Y, ZH, CORE = AXES
CUTS = ((0, 96), (96, 100))
HALF = 48
COLOURS = ((X, Y), (Y, X))
BOTH = (0, 1)
ORDER = (2, 1, 3, 0)


def slot_of(block, colour):
    x, z, y = block >> 3, (block >> 2) & 1, block & 3
    if colour == 0:
        return x * 8 + y * 2 + z
    return y * 8 + x * 2 + z


def block_in(slot, colour):
    p, q, z = slot >> 3, (slot >> 1) & 3, slot & 1
    if colour == 0:
        return p * 8 + z * 4 + q
    return q * 8 + z * 4 + p


def split_pair(value):
    high = value.astype(jnp.bfloat16)
    low = (value - high.astype(jnp.float32)).astype(jnp.bfloat16)
    return jnp.concatenate([high, low], axis=1)


def stacked_tile(tile):
    row = split_pair(tile)
    return jnp.concatenate([row, row], axis=0)


def full_product(left, right):
    both = jnp.dot(left, right, preferred_element_type=jnp.float32)
    return both[:, :TILE] + both[:, TILE:]


def tile_copies(tiles, held, sems):
    part = CAP // TILE_DMAS
    return [
        pltpu.make_async_copy(
            tiles.at[pl.ds(i * part, part)], held.at[pl.ds(i * part, part)], sems.at[i]
        )
        for i in range(TILE_DMAS)
    ]


def shifted(axis, step):
    size = SIZES[axis]
    return lax.rem(lax.axis_index(axis) + (step + size), size)


def chain(targets, count):
    row = lax.broadcasted_iota(jnp.int32, (CAP, CAP), 0)
    lane = lax.broadcasted_iota(jnp.int32, (CAP, CAP), 1)
    along = jnp.broadcast_to(targets, (CAP, CAP))
    down = jnp.sum(jnp.where(row == lane, along, 0), axis=1, keepdims=True)
    live = lane < count
    before = jnp.max(jnp.where(live & (lane < row) & (along == down), lane, -1), axis=1, keepdims=True)
    last = jnp.max(jnp.where(live & (along == row), lane, -1), axis=1, keepdims=True)
    return jnp.where(before < 0, NONE, before), jnp.where(last < 0, NONE, last)


class Sender:
    def __init__(self, send_sems, recv_sems):
        self.send_sems, self.recv_sems, self.count, self.sent = send_sems, recv_sems, 0, []

    def start(self, src, dst, where):
        i = self.count
        self.count += 1
        copy = pltpu.make_async_remote_copy(
            src_ref=src,
            dst_ref=dst,
            send_sem=self.send_sems.at[i],
            recv_sem=self.recv_sems.at[i],
            device_id=where,
            device_id_type=MESH,
        )
        copy.start()
        self.sent.append(copy)
        return copy

    def along(self, block, axis, step):
        return self.start(block, block, {axis: shifted(axis, step)})

    def finish(self):
        for copy in self.sent:
            copy.wait_send()


class RingSum:
    def __init__(self, sender, axis, part, landed, total):
        self.s, self.axis, self.part, self.landed, self.total = sender, axis, part, landed, total
        self.right, self.left = {axis: shifted(axis, 1)}, {axis: shifted(axis, -1)}

    def begin_far(self):
        opposite = shifted(self.axis, 2)
        self.r1 = self.s.start(self.part(opposite, 0), self.landed(0), self.right)
        self.l1 = self.s.start(self.part(opposite, 1), self.landed(1), self.left)

    def begin_right(self):
        self.r2 = self.s.start(self.part(self.right[self.axis], 1), self.landed(2), self.right)

    def begin_left(self):
        self.l2 = self.s.start(self.part(self.left[self.axis], 0), self.landed(3), self.left)

    def begin(self):
        self.begin_far()
        self.begin_right()
        self.begin_left()

    def middle_right(self):
        self.r1.wait_recv()
        self.landed(0)[...] = self.landed(0)[...] + self.part(self.right[self.axis], 0)[...]
        self.r3 = self.s.start(self.landed(0), self.landed(4), self.right)

    def middle_left(self):
        self.l1.wait_recv()
        self.landed(1)[...] = self.landed(1)[...] + self.part(self.left[self.axis], 1)[...]
        self.l3 = self.s.start(self.landed(1), self.landed(5), self.left)

    def middle(self):
        self.middle_right()
        self.middle_left()

    def end(self):
        me = lax.axis_index(self.axis)
        landed, part = self.landed, self.part
        self.r2.wait_recv()
        self.l2.wait_recv()
        self.r3.wait_recv()
        self.total(0)[...] = (part(me, 0)[...] + landed(3)[...]) + landed(4)[...]
        self.l3.wait_recv()
        self.total(1)[...] = (part(me, 1)[...] + landed(2)[...]) + landed(5)[...]


def part_rows(ref, h, rows):
    return ref.at[pl.ds(h * HALF, rows - HALF if h else HALF)]


def whole_kernel(
    enc_src_any,
    enc_hid_any,
    enc_count,
    dec_src_any,
    dec_hid_any,
    dec_count,
    field_any,
    gain_any,
    enc_tiles,
    dec_tiles,
    result_0,
    result_1,
    rms,
    enc_src,
    enc_hid,
    dec_src,
    dec_hid,
    field,
    gain,
    enc_held,
    dec_held,
    table,
    table_s,
    blocks,
    left,
    right,
    sums,
    partial,
    first_in,
    first_sum,
    pair_in,
    pair_sum,
    second_in,
    hidden,
    back,
    core_in,
    core_sum,
    ring_in,
    squares,
    square_in,
    local_sems,
    send_sems,
    recv_sems,
):
    result = (result_0, result_1)
    x, y, z = lax.axis_index(X), lax.axis_index(Y), lax.axis_index(Z)
    zh, core = lax.axis_index(ZH), lax.axis_index(CORE)
    other, twin = 1 - z, 1 - core
    where = {X: x, Y: y}

    plane = [
        {X: shifted(X, dx), Y: shifted(Y, dy)} for dx in range(4) for dy in range(4) if dx + dy
    ]
    stack = [
        {Z: lax.rem(z + dz, 2), ZH: lax.rem(zh + dh, 4), CORE: lax.rem(core + dc, 2)}
        for dz in range(2)
        for dh in range(4)
        for dc in range(2)
        if dz + dh + dc
    ]
    peers = plane + stack
    barrier = pltpu.get_barrier_semaphore()
    small = [
        pltpu.make_async_copy(there, here, local_sems.at[2, i])
        for i, (there, here) in enumerate(
            (
                (enc_src_any, enc_src),
                (enc_hid_any, enc_hid),
                (dec_src_any, dec_src),
                (dec_hid_any, dec_hid),
                (gain_any, gain),
            )
        )
    ]
    field_copy = pltpu.make_async_copy(field_any, field, local_sems.at[2, 7])
    enc_copies = tile_copies(enc_tiles, enc_held, local_sems.at[0])
    dec_copies = tile_copies(dec_tiles, dec_held, local_sems.at[1])
    for copy in (*small, field_copy, *enc_copies):
        copy.start()
    for peer in peers:
        pl.semaphore_signal(barrier, inc=1, device_id=peer, device_id_type=MESH)

    sums[NONE] = jnp.zeros((ROWS, TILE), jnp.float32)
    for copy in small:
        copy.wait()
    before, last = chain(enc_hid[...] & (HID_BLK - 1), enc_count[0])
    before_back, last_back = chain(dec_src[...] & (SRC_BLK - 1), dec_count[0])
    lane = lax.broadcasted_iota(jnp.int32, (CAP, TILE), 1)
    table[...] = jnp.where(
        lane == 0, before, jnp.where(lane == 1, last, jnp.where(lane == 2, before_back, last_back))
    )
    table_copy = pltpu.make_async_copy(table, table_s, local_sems.at[3, 0])
    field_copy.wait()
    for i in range(SRC_BLK):
        value = field[i * ROWS : (i + 1) * ROWS]
        blocks[i] = value
        left[i] = split_pair(value)
        if i == 1:
            table_copy.start()
    for copy in dec_copies:
        copy.start()
    table_copy.wait()
    for chunk, copy in enumerate(enc_copies):
        copy.wait()

        @pl.loop(0, CAP // TILE_DMAS // UNROLL)
        def _(step, chunk=chunk):
            for i in range(UNROLL):
                k = chunk * (CAP // TILE_DMAS) + step * UNROLL + i
                product = full_product(left[enc_src[k] & (SRC_BLK - 1)], stacked_tile(enc_held[k]))
                sums[k] = sums[table_s[k, 0]] + product

    @pl.loop(0, HID_BLK)
    def _(slot):
        for c in BOTH:
            start, rows = CUTS[c]
            partial[c][slot] = sums[table_s[block_in(slot, c), 1], start : start + rows]

    pl.semaphore_wait(barrier, len(peers))
    s = Sender(send_sems, recv_sems)
    row = lax.broadcasted_iota(jnp.int32, (ROWS, CH), 0)
    column = lax.broadcasted_iota(jnp.int32, (ROWS, CH), 1)
    scale = jnp.sum(
        jnp.where((row >> 1) == column, jnp.broadcast_to(gain[...], (ROWS, CH)), 0.0),
        axis=1,
        keepdims=True,
    )

    def reduce_steps():
        def first_ring(c, i):
            p, q = COLOURS[c]
            there = shifted(q, ORDER[i])
            return RingSum(
                s,
                p,
                lambda m, h: partial[c].at[m * 8 + there * 2 + h],
                lambda n: first_in[c].at[i, n],
                lambda h: first_sum[c].at[there * 2 + h],
            )

        first = [[first_ring(c, i) for i in range(4)] for c in BOTH]
        pairs, second = {}, {}

        def settle(i):
            for c in BOTH:
                first[c][i].end()
                there = shifted(COLOURS[c][1], ORDER[i])
                pairs[c, i] = s.start(
                    first_sum[c].at[there * 2 + other], pair_in[c].at[there], {Z: other}
                )

        def pair_back(c, i):
            there = shifted(COLOURS[c][1], ORDER[i])
            pairs[c, i].wait_recv()
            pair_sum[c][there] = first_sum[c][there * 2 + z] + pair_in[c][there]
            if i < 3:
                second[c, i] = s.start(pair_sum[c].at[there], second_in[c].at[i], {COLOURS[c][1]: there})

        for i in (0, 1):
            for c in BOTH:
                first[c][i].begin()
        yield
        for c in BOTH:
            first[c][0].middle()
            first[c][2].begin()
        yield
        for c in BOTH:
            first[c][1].middle()
            first[c][3].begin()
        settle(0)
        yield
        for c in BOTH:
            first[c][2].middle()
        settle(1)
        for c in BOTH:
            pair_back(c, 0)
        yield
        for c in BOTH:
            first[c][3].middle()
        settle(2)
        for c in BOTH:
            pair_back(c, 1)
        yield
        settle(3)
        for c in BOTH:
            pair_back(c, 2)
        yield
        evens, odds, values = [], [], []
        for c in BOTH:
            pair_back(c, 3)
            value = pair_sum[c][where[COLOURS[c][1]]]
            for i in range(3):
                second[c, i].wait_recv()
                value = value + second_in[c][i]
            values.append(value)
            parity = lax.broadcasted_iota(jnp.int32, value.shape, 0) & 1
            square = value * value
            evens.append(jnp.sum(jnp.where(parity == 0, square, 0.0), axis=0, keepdims=True))
            odds.append(jnp.sum(jnp.where(parity == 1, square, 0.0), axis=0, keepdims=True))
        even = lax.rsqrt((evens[0] + evens[1]) * (1.0 / CH) + EPSILON)
        odd = lax.rsqrt((odds[0] + odds[1]) * (1.0 / CH) + EPSILON)
        for c in BOTH:
            start, rows = CUTS[c]
            parity = lax.broadcasted_iota(jnp.int32, (rows, TILE), 0) & 1
            p, q = (where[axis] for axis in COLOURS[c])
            hidden[c][p * 8 + q * 2 + z] = (
                values[c] * scale[start : start + rows] * jnp.where(parity == 0, even, odd)
            )

    def gather_steps():
        inner, paired, outer, passed = {}, {}, {}, {}

        def outer_block(c, m, step, far):
            there = shifted(COLOURS[c][1], step)
            return hidden[c].at[m * 8 + there * 2 + (other if far else z)]

        def inner_block(c, step):
            p, q = COLOURS[c]
            return hidden[c].at[where[p] * 8 + shifted(q, step) * 2 + z]

        def to_pair(c, step):
            paired[c, step] = s.along(inner_block(c, step), Z, 1)

        def to_line(c, step, far):
            p = COLOURS[c][0]
            block = outer_block(c, where[p], step, far)
            outer[c, step, far] = [s.along(block, p, 1), s.along(block, p, -1)]

        def along_line(c, step, far):
            p = COLOURS[c][0]
            from_left, from_right = outer[c, step, far]
            if far:
                from_right.wait_recv()
                passed[c, step, far] = s.along(outer_block(c, shifted(p, 1), step, far), p, -1)
            else:
                from_left.wait_recv()
                passed[c, step, far] = s.along(outer_block(c, shifted(p, -1), step, far), p, 1)

        for c in BOTH:
            q, mine = COLOURS[c][1], inner_block(c, 0)
            for step in (1, 3, 2):
                inner[c, step] = s.along(mine, q, step)
            to_pair(c, 0)
        for c in BOTH:
            to_line(c, 0, False)
        yield
        for step in (1, 3, 2):
            for c in BOTH:
                inner[c, step].wait_recv()
                to_pair(c, 4 - step)
                to_line(c, 4 - step, False)
        yield
        for c in BOTH:
            paired[c, 0].wait_recv()
            to_line(c, 0, True)
        yield
        for c in BOTH:
            along_line(c, 0, False)
        yield
        for step in (3, 1, 2):
            for c in BOTH:
                paired[c, step].wait_recv()
                to_line(c, step, True)
        yield
        for step, far in ((3, False), (1, False), (0, True), (2, False), (3, True), (1, True), (2, True)):
            for c in BOTH:
                along_line(c, step, far)
        yield
        for c, step, far in passed:
            outer[c, step, far][0 if far else 1].wait_recv()
            passed[c, step, far].wait_recv()

    def decode(c):
        here = slice(CUTS[c][0], CUTS[c][0] + CUTS[c][1])

        @pl.loop(0, CAP // UNROLL)
        def _(step):
            for i in range(UNROLL):
                k = step * UNROLL + i
                block = dec_hid[k] & (HID_BLK - 1)
                product = full_product(split_pair(hidden[c][slot_of(block, c)]), right[k])
                sums[k, here] = sums[table_s[k, 2], here] + product

        @pl.loop(0, SRC_BLK)
        def _(i):
            back[c][i] = sums[table_s[i, 3], here]

    def column_steps(c):
        rows = CUTS[c][1]
        crossing = {}
        for step in ORDER:
            m = lax.rem(zh + step, 4)
            crossing[step] = s.start(back[c].at[twin * 4 + m], core_in[c].at[m], {CORE: twin})
        yield
        ring = RingSum(
            s,
            ZH,
            lambda m, h: part_rows(core_sum[c].at[m], h, rows),
            lambda n: ring_in[c].at[n, pl.ds(0, rows - HALF if n in (1, 2, 5) else HALF)],
            lambda h: part_rows(result[c].at[core * 4 + zh], h, rows),
        )
        for step in ORDER:
            m = lax.rem(zh + step, 4)
            crossing[step].wait_recv()
            core_sum[c][m] = back[c][core * 4 + m] + core_in[c][m]
            if step == 2:
                ring.begin_far()
            elif step == 1:
                ring.begin_right()
            elif step == 3:
                ring.begin_left()
        yield
        ring.middle()
        yield
        ring.end()

        def own_half(step, h):
            return part_rows(result[c].at[core * 4 + lax.rem(zh + step, 4)], h, rows)

        def to_twin(step, h):
            return s.along(own_half(step, h), CORE, 1)

        to_right = [s.along(own_half(0, 0), ZH, 1)]
        to_left = [s.along(own_half(0, 1), ZH, -1)]
        to_right.append(s.along(own_half(0, 1), ZH, 1))
        to_left.append(s.along(own_half(0, 0), ZH, -1))
        twins = [s.along(result[c].at[core * 4 + zh], CORE, 1)]
        yield
        to_right[0].wait_recv()
        passing = [s.along(own_half(3, 0), ZH, 1)]
        to_left[0].wait_recv()
        passing.append(s.along(own_half(1, 1), ZH, -1))
        twins += [to_twin(3, 0), to_twin(1, 1)]
        yield
        to_right[1].wait_recv()
        to_left[1].wait_recv()
        twins += [to_twin(3, 1), to_twin(1, 0)]
        for h in BOTH:
            passing[h].wait_recv()
            twins.append(to_twin(2, h))
        yield
        for copy in twins:
            copy.wait_recv()

    def own_squares(c):
        start, rows = CUTS[c]
        error = result[c][core * 4 + zh] - blocks[core * 4 + zh, start : start + rows]
        by_row = jnp.sum(error * error, axis=1, keepdims=True)
        row = start + lax.broadcasted_iota(jnp.int32, (rows, TILE), 0)
        column = lax.broadcasted_iota(jnp.int32, (rows, TILE), 1)
        line = jnp.sum(jnp.where((row >> 1) == column, by_row, 0.0), axis=0, keepdims=True)
        return jnp.broadcast_to(line, (8, TILE))

    def exchange(stage, first_slot, those):
        return [
            s.start(squares.at[stage], square_in.at[first_slot + i], peer)
            for i, peer in enumerate(those)
        ]

    def collect(stage, first_slot, copies):
        value = squares[stage]
        for i, copy in enumerate(copies):
            copy.wait_recv()
            value = value + square_in[first_slot + i]
        squares[stage + 1] = value

    columns = [column_steps(c) for c in BOTH]
    reduce, gather = reduce_steps(), gather_steps()

    def go(*those):
        for steps in those:
            next(steps, None)

    z0, z1 = columns
    go(reduce)
    for copy in dec_copies:
        copy.wait()

    @pl.loop(0, CAP)
    def _(k):
        right[k] = stacked_tile(dec_held[k])

    for steps in (reduce, gather):
        for _ in steps:
            pass
    decode(0)
    go(z0)
    decode(1)
    go(z1, z0, z1, z0, z1, z0, z1)
    line = own_squares(0)
    go(z0)
    squares[0] = line + own_squares(1)
    copies = exchange(0, 0, plane)
    go(z1)
    collect(0, 0, copies)
    copies = exchange(1, 15, stack)
    go(z0, z1)
    collect(1, 15, copies)
    rms[...] = jnp.sqrt(squares[2] * (1.0 / TOTAL_POINTS) + EPSILON)
    go(z0, z1)
    assert s.count == N_SEMS
    s.finish()


def assemble_kernel(result_0, result_1, rms, out, rms_out):
    for i in range(SRC_BLK):
        for (start, rows), part in zip(CUTS, (result_0, result_1)):
            out[i * ROWS + start : i * ROWS + start + rows] = part[i]
    rms_out[...] = rms[0:1, 0:CH]


VMEM = pl.BlockSpec(memory_space=pltpu.VMEM)
HBM = pl.BlockSpec(memory_space=pltpu.HBM)
SMEM = pl.BlockSpec(memory_space=pltpu.SMEM)


def coloured(*lead):
    return [pltpu.VMEM((*lead, rows, TILE), jnp.float32) for _, rows in CUTS]


def body(
    source_field,
    hidden_gain,
    enc_tiles,
    enc_src_block,
    enc_hid_block,
    enc_count,
    dec_tiles,
    dec_src_block,
    dec_hid_block,
    dec_count,
):
    rows = source_field.transpose(0, 2, 1, 3).reshape(SRC_BLK * ROWS, TILE)
    held = pltpu.VMEM((CAP, TILE, TILE), jnp.float32)
    parts = pl.pallas_call(
        whole_kernel,
        out_shape=(
            *coloured(SRC_BLK),
            pltpu.VMEM((8, TILE), jnp.float32),
        ),
        in_specs=[HBM, HBM, SMEM, HBM, HBM, SMEM, HBM, HBM, HBM, HBM],
        out_specs=(VMEM,) * 3,
        scratch_shapes=[
            pltpu.SMEM((CAP,), jnp.int32),
            pltpu.VMEM((1, CAP), jnp.int32),
            pltpu.VMEM((1, CAP), jnp.int32),
            pltpu.SMEM((CAP,), jnp.int32),
            pltpu.VMEM((SRC_BLK * ROWS, TILE), jnp.float32),
            pltpu.VMEM((1, CH), jnp.float32),
            held,
            held,
            pltpu.VMEM((CAP, TILE), jnp.int32),
            pltpu.SMEM((CAP, TILE), jnp.int32),
            pltpu.VMEM((SRC_BLK, ROWS, TILE), jnp.float32),
            pltpu.VMEM((SRC_BLK, ROWS, 2 * TILE), jnp.bfloat16),
            pltpu.VMEM((CAP, 2 * TILE, 2 * TILE), jnp.bfloat16),
            pltpu.VMEM((CAP + 1, ROWS, TILE), jnp.float32),
            coloured(HID_BLK),
            coloured(4, 6),
            coloured(8),
            coloured(4),
            coloured(4),
            coloured(3),
            coloured(HID_BLK),
            coloured(SRC_BLK),
            coloured(4),
            coloured(4),
            [pltpu.VMEM((6, 56, TILE), jnp.float32)] * 2,
            pltpu.VMEM((3, 8, TILE), jnp.float32),
            pltpu.VMEM((30, 8, TILE), jnp.float32),
            pltpu.SemaphoreType.DMA((4, 8)),
            pltpu.SemaphoreType.DMA((N_SEMS,)),
            pltpu.SemaphoreType.DMA((N_SEMS,)),
        ],
        compiler_params=pltpu.CompilerParams(collective_id=0, has_side_effects=True),
    )(
        enc_src_block,
        enc_hid_block.reshape(1, CAP),
        enc_count,
        dec_src_block.reshape(1, CAP),
        dec_hid_block,
        dec_count,
        rows,
        hidden_gain.reshape(1, CH),
        enc_tiles,
        dec_tiles,
    )
    returned, rms = pl.pallas_call(
        assemble_kernel,
        out_shape=(
            jax.ShapeDtypeStruct((SRC_BLK * ROWS, TILE), jnp.float32),
            jax.ShapeDtypeStruct((1, CH), jnp.float32),
        ),
        in_specs=[VMEM] * 3,
        out_specs=(VMEM, VMEM),
    )(*[pltpu.with_memory_space_constraint(part, pltpu.VMEM) for part in parts])
    returned = returned.reshape(SRC_BLK, CH, BATCH, TILE).transpose(0, 2, 1, 3)
    return returned, rms.reshape(CH)


def solution(mesh):
    split = Mesh(mesh.devices.reshape(4, 2, 4, 4, 2), AXES)
    every = P(AXES)
    in_specs = (
        P(SRC, None, None, None),
        P(),
        P(AXES, None, None),
        every,
        every,
        every,
        P(AXES, None, None),
        every,
        every,
        every,
    )
    out_specs = (P(SRC, None, None, None), P())
    return jax.shard_map(body, mesh=split, in_specs=in_specs, out_specs=out_specs, check_vma=False)
```

```python
import jax
import jax.numpy as jnp
from jax import lax
from jax.experimental import pallas as pl
from jax.experimental.pallas import tpu as pltpu
from jax.sharding import Mesh
from jax.sharding import PartitionSpec as P

CH = 98
BATCH = 2
TILE = 128
ROWS = CH * BATCH
SRC_BLK = 8
HID_BLK = 32
CAP = 32
NONE = CAP
TOTAL_POINTS = 256 * BATCH * TILE
EPSILON = 1e-06
AXES = ("src_0", "src_1", "src_2", "hid_0", "hid_1")
SRC = ("src_0", "src_1", "src_2")
SIZES = {"src_0": 4, "src_1": 2, "src_2": 4, "hid_0": 4, "hid_1": 2}
MESH = pl.DeviceIdType.MESH
TILE_DMAS = 2
UNROLL = 16
N_SEMS = 188

X, Z, Y, ZH, CORE = AXES
CUTS = ((0, 96), (96, 100))
HALF = 48
COLOURS = ((X, Y), (Y, X))
BOTH = (0, 1)
ORDER = (2, 1, 3, 0)


def slot_of(block, colour):
    x, z, y = block >> 3, (block >> 2) & 1, block & 3
    if colour == 0:
        return x * 8 + y * 2 + z
    return y * 8 + x * 2 + z


def block_in(slot, colour):
    p, q, z = slot >> 3, (slot >> 1) & 3, slot & 1
    if colour == 0:
        return p * 8 + z * 4 + q
    return q * 8 + z * 4 + p


def split_pair(value):
    high = value.astype(jnp.bfloat16)
    low = (value - high.astype(jnp.float32)).astype(jnp.bfloat16)
    return jnp.concatenate([high, low], axis=1)


def stacked_tile(tile):
    row = split_pair(tile)
    return jnp.concatenate([row, row], axis=0)


def full_product(left, right):
    both = jnp.dot(left, right, preferred_element_type=jnp.float32)
    return both[:, :TILE] + both[:, TILE:]


def tile_copies(tiles, held, sems):
    part = CAP // TILE_DMAS
    return [
        pltpu.make_async_copy(
            tiles.at[pl.ds(i * part, part)], held.at[pl.ds(i * part, part)], sems.at[i]
        )
        for i in range(TILE_DMAS)
    ]


def shifted(axis, step):
    size = SIZES[axis]
    return lax.rem(lax.axis_index(axis) + (step + size), size)


def chain(targets, count):
    row = lax.broadcasted_iota(jnp.int32, (CAP, CAP), 0)
    lane = lax.broadcasted_iota(jnp.int32, (CAP, CAP), 1)
    along = jnp.broadcast_to(targets, (CAP, CAP))
    down = jnp.sum(jnp.where(row == lane, along, 0), axis=1, keepdims=True)
    live = lane < count
    before = jnp.max(jnp.where(live & (lane < row) & (along == down), lane, -1), axis=1, keepdims=True)
    last = jnp.max(jnp.where(live & (along == row), lane, -1), axis=1, keepdims=True)
    return jnp.where(before < 0, NONE, before), jnp.where(last < 0, NONE, last)


class Sender:
    def __init__(self, send_sems, recv_sems):
        self.send_sems, self.recv_sems, self.count, self.sent = send_sems, recv_sems, 0, []

    def start(self, src, dst, where):
        i = self.count
        self.count += 1
        copy = pltpu.make_async_remote_copy(
            src_ref=src,
            dst_ref=dst,
            send_sem=self.send_sems.at[i],
            recv_sem=self.recv_sems.at[i],
            device_id=where,
            device_id_type=MESH,
        )
        copy.start()
        self.sent.append(copy)
        return copy

    def along(self, block, axis, step):
        return self.start(block, block, {axis: shifted(axis, step)})

    def finish(self):
        for copy in self.sent:
            copy.wait_send()


class RingSum:
    def __init__(self, sender, axis, part, landed, total):
        self.s, self.axis, self.part, self.landed, self.total = sender, axis, part, landed, total
        self.right, self.left = {axis: shifted(axis, 1)}, {axis: shifted(axis, -1)}

    def begin_far(self):
        opposite = shifted(self.axis, 2)
        self.r1 = self.s.start(self.part(opposite, 0), self.landed(0), self.right)
        self.l1 = self.s.start(self.part(opposite, 1), self.landed(1), self.left)

    def begin_right(self):
        self.r2 = self.s.start(self.part(self.right[self.axis], 1), self.landed(2), self.right)

    def begin_left(self):
        self.l2 = self.s.start(self.part(self.left[self.axis], 0), self.landed(3), self.left)

    def begin(self):
        self.begin_far()
        self.begin_right()
        self.begin_left()

    def middle_right(self):
        self.r1.wait_recv()
        self.landed(0)[...] = self.landed(0)[...] + self.part(self.right[self.axis], 0)[...]
        self.r3 = self.s.start(self.landed(0), self.landed(4), self.right)

    def middle_left(self):
        self.l1.wait_recv()
        self.landed(1)[...] = self.landed(1)[...] + self.part(self.left[self.axis], 1)[...]
        self.l3 = self.s.start(self.landed(1), self.landed(5), self.left)

    def middle(self):
        self.middle_right()
        self.middle_left()

    def end(self):
        me = lax.axis_index(self.axis)
        landed, part = self.landed, self.part
        self.r2.wait_recv()
        self.l2.wait_recv()
        self.r3.wait_recv()
        self.total(0)[...] = (part(me, 0)[...] + landed(3)[...]) + landed(4)[...]
        self.l3.wait_recv()
        self.total(1)[...] = (part(me, 1)[...] + landed(2)[...]) + landed(5)[...]


def whole_kernel(
    enc_src_any,
    enc_hid_any,
    enc_count,
    dec_src_any,
    dec_hid_any,
    dec_count,
    field_any,
    gain_any,
    enc_tiles,
    dec_tiles,
    result_0,
    result_1,
    rms,
    enc_src,
    enc_hid,
    dec_src,
    dec_hid,
    field,
    gain,
    enc_held,
    dec_held,
    table,
    table_s,
    blocks,
    left,
    right,
    sums,
    partial,
    first_in,
    first_sum,
    pair_in,
    pair_sum,
    second_in,
    hidden,
    back,
    core_in,
    core_sum,
    ring_in,
    squares,
    square_in,
    local_sems,
    send_sems,
    recv_sems,
):
    result = (result_0, result_1)
    x, y, z = lax.axis_index(X), lax.axis_index(Y), lax.axis_index(Z)
    zh, core = lax.axis_index(ZH), lax.axis_index(CORE)
    other, twin = 1 - z, 1 - core
    where = {X: x, Y: y}

    plane = [
        {X: shifted(X, dx), Y: shifted(Y, dy)} for dx in range(4) for dy in range(4) if dx + dy
    ]
    stack = [
        {Z: lax.rem(z + dz, 2), ZH: lax.rem(zh + dh, 4), CORE: lax.rem(core + dc, 2)}
        for dz in range(2)
        for dh in range(4)
        for dc in range(2)
        if dz + dh + dc
    ]
    peers = plane + stack
    barrier = pltpu.get_barrier_semaphore()
    small = [
        pltpu.make_async_copy(there, here, local_sems.at[2, i])
        for i, (there, here) in enumerate(
            (
                (enc_src_any, enc_src),
                (enc_hid_any, enc_hid),
                (dec_src_any, dec_src),
                (dec_hid_any, dec_hid),
                (gain_any, gain),
            )
        )
    ]
    field_copy = pltpu.make_async_copy(field_any, field, local_sems.at[2, 7])
    enc_copies = tile_copies(enc_tiles, enc_held, local_sems.at[0])
    dec_copies = tile_copies(dec_tiles, dec_held, local_sems.at[1])
    for copy in (*small, field_copy, *enc_copies):
        copy.start()
    for peer in peers:
        pl.semaphore_signal(barrier, inc=1, device_id=peer, device_id_type=MESH)

    sums[NONE] = jnp.zeros((ROWS, TILE), jnp.float32)
    for copy in small:
        copy.wait()
    before, last = chain(enc_hid[...] & (HID_BLK - 1), enc_count[0])
    before_back, last_back = chain(dec_src[...] & (SRC_BLK - 1), dec_count[0])
    lane = lax.broadcasted_iota(jnp.int32, (CAP, TILE), 1)
    table[...] = jnp.where(
        lane == 0, before, jnp.where(lane == 1, last, jnp.where(lane == 2, before_back, last_back))
    )
    table_copy = pltpu.make_async_copy(table, table_s, local_sems.at[3, 0])
    field_copy.wait()
    for i in range(SRC_BLK):
        value = field[i * ROWS : (i + 1) * ROWS]
        blocks[i] = value
        left[i] = split_pair(value)
        if i == 1:
            table_copy.start()
    for copy in dec_copies:
        copy.start()
    table_copy.wait()
    for chunk, copy in enumerate(enc_copies):
        copy.wait()

        @pl.loop(0, CAP // TILE_DMAS // UNROLL)
        def _(step, chunk=chunk):
            for i in range(UNROLL):
                k = chunk * (CAP // TILE_DMAS) + step * UNROLL + i
                product = full_product(left[enc_src[k] & (SRC_BLK - 1)], stacked_tile(enc_held[k]))
                sums[k] = sums[table_s[k, 0]] + product

    @pl.loop(0, HID_BLK)
    def _(slot):
        for c in BOTH:
            start, rows = CUTS[c]
            partial[c][slot] = sums[table_s[block_in(slot, c), 1], start : start + rows]

    pl.semaphore_wait(barrier, len(peers))
    s = Sender(send_sems, recv_sems)
    row = lax.broadcasted_iota(jnp.int32, (ROWS, CH), 0)
    column = lax.broadcasted_iota(jnp.int32, (ROWS, CH), 1)
    scale = jnp.sum(
        jnp.where((row >> 1) == column, jnp.broadcast_to(gain[...], (ROWS, CH)), 0.0),
        axis=1,
        keepdims=True,
    )

    def reduce_steps():
        def first_ring(c, i):
            p, q = COLOURS[c]
            there = shifted(q, ORDER[i])
            return RingSum(
                s,
                p,
                lambda m, h: partial[c].at[m * 8 + there * 2 + h],
                lambda n: first_in[c].at[i, n],
                lambda h: first_sum[c].at[there * 2 + h],
            )

        first = [[first_ring(c, i) for i in range(4)] for c in BOTH]
        pairs, second = {}, {}

        def settle(i):
            for c in BOTH:
                first[c][i].end()
                there = shifted(COLOURS[c][1], ORDER[i])
                pairs[c, i] = s.start(
                    first_sum[c].at[there * 2 + other], pair_in[c].at[there], {Z: other}
                )

        def pair_back(c, i):
            there = shifted(COLOURS[c][1], ORDER[i])
            pairs[c, i].wait_recv()
            pair_sum[c][there] = first_sum[c][there * 2 + z] + pair_in[c][there]
            if i < 3:
                second[c, i] = s.start(pair_sum[c].at[there], second_in[c].at[i], {COLOURS[c][1]: there})

        for c in BOTH:
            first[c][0].begin()
        for c in BOTH:
            first[c][1].begin_far()
        yield
        for c in BOTH:
            first[c][0].middle()
            first[c][2].begin_far()
            first[c][1].begin_right()
            first[c][1].begin_left()
        yield
        for c in BOTH:
            first[c][1].middle()
            first[c][3].begin_far()
            first[c][2].begin_right()
            first[c][2].begin_left()
        settle(0)
        yield
        for c in BOTH:
            first[c][2].middle()
            first[c][3].begin_right()
            first[c][3].begin_left()
        settle(1)
        for c in BOTH:
            pair_back(c, 0)
        yield
        for c in BOTH:
            first[c][3].middle()
        settle(2)
        for c in BOTH:
            pair_back(c, 1)
        yield
        settle(3)
        for c in BOTH:
            pair_back(c, 2)
        yield
        evens, odds, values = [], [], []
        for c in BOTH:
            pair_back(c, 3)
            value = pair_sum[c][where[COLOURS[c][1]]]
            for i in range(3):
                second[c, i].wait_recv()
                value = value + second_in[c][i]
            values.append(value)
            parity = lax.broadcasted_iota(jnp.int32, value.shape, 0) & 1
            square = value * value
            evens.append(jnp.sum(jnp.where(parity == 0, square, 0.0), axis=0, keepdims=True))
            odds.append(jnp.sum(jnp.where(parity == 1, square, 0.0), axis=0, keepdims=True))
        even = lax.rsqrt((evens[0] + evens[1]) * (1.0 / CH) + EPSILON)
        odd = lax.rsqrt((odds[0] + odds[1]) * (1.0 / CH) + EPSILON)
        for c in BOTH:
            start, rows = CUTS[c]
            parity = lax.broadcasted_iota(jnp.int32, (rows, TILE), 0) & 1
            p, q = (where[axis] for axis in COLOURS[c])
            hidden[c][p * 8 + q * 2 + z] = (
                values[c] * scale[start : start + rows] * jnp.where(parity == 0, even, odd)
            )

    def gather_steps():
        inner, paired, outer, passed = {}, {}, {}, {}

        def outer_block(c, m, step, far):
            there = shifted(COLOURS[c][1], step)
            return hidden[c].at[m * 8 + there * 2 + (other if far else z)]

        def inner_block(c, step):
            p, q = COLOURS[c]
            return hidden[c].at[where[p] * 8 + shifted(q, step) * 2 + z]

        def to_pair(c, step):
            paired[c, step] = s.along(inner_block(c, step), Z, 1)

        def to_line(c, step, far):
            p = COLOURS[c][0]
            block = outer_block(c, where[p], step, far)
            outer[c, step, far] = [s.along(block, p, 1), s.along(block, p, -1)]

        def along_line(c, step, far):
            p = COLOURS[c][0]
            from_left, from_right = outer[c, step, far]
            if far:
                from_right.wait_recv()
                passed[c, step, far] = s.along(outer_block(c, shifted(p, 1), step, far), p, -1)
            else:
                from_left.wait_recv()
                passed[c, step, far] = s.along(outer_block(c, shifted(p, -1), step, far), p, 1)

        for c in BOTH:
            q, mine = COLOURS[c][1], inner_block(c, 0)
            for step in (1, 3, 2):
                inner[c, step] = s.along(mine, q, step)
            to_pair(c, 0)
        for c in BOTH:
            to_line(c, 0, False)
        yield
        for step in (1, 3, 2):
            for c in BOTH:
                inner[c, step].wait_recv()
                to_pair(c, 4 - step)
                to_line(c, 4 - step, False)
        yield
        for c in BOTH:
            paired[c, 0].wait_recv()
            to_line(c, 0, True)
        yield
        for c in BOTH:
            along_line(c, 0, False)
        yield
        for step in (3, 1, 2):
            for c in BOTH:
                paired[c, step].wait_recv()
                to_line(c, step, True)
        yield
        for step, far in ((3, False), (1, False), (0, True), (2, False), (3, True), (1, True), (2, True)):
            for c in BOTH:
                along_line(c, step, far)
        yield
        for c, step, far in passed:
            outer[c, step, far][0 if far else 1].wait_recv()
            passed[c, step, far].wait_recv()

    def decode():
        for k in range(CAP):
            block = dec_hid[k] & (HID_BLK - 1)
            split = [split_pair(hidden[c][slot_of(block, c)]) for c in BOTH]
            product = full_product(jnp.concatenate(split, axis=0), right[k])
            sums[k] = sums[table_s[k, 2]] + product

        @pl.loop(0, SRC_BLK)
        def _(i):
            for c in BOTH:
                start, rows = CUTS[c]
                back[c][i] = sums[table_s[i, 3], start : start + rows]

    def column_steps(c):
        crossing, column, twins = {}, {}, []
        rows = CUTS[c][1]

        def half_of(block, h):
            return block.at[pl.ds(h * HALF, rows - HALF if h else HALF)]

        ring = RingSum(
            s,
            ZH,
            lambda m, h: half_of(core_sum[c].at[m], h),
            lambda n: ring_in[c].at[n, pl.ds(0, rows - HALF if n in (1, 2, 5) else HALF)],
            lambda h: half_of(result[c].at[core * 4 + zh], h),
        )
        for step in ORDER:
            m = lax.rem(zh + step, 4)
            crossing[step] = s.start(back[c].at[twin * 4 + m], core_in[c].at[m], {CORE: twin})
        yield
        for step in ORDER:
            m = lax.rem(zh + step, 4)
            crossing[step].wait_recv()
            core_sum[c][m] = back[c][core * 4 + m] + core_in[c][m]
            if step == 2:
                ring.begin_far()
            elif step == 1:
                ring.begin_right()
            elif step == 3:
                ring.begin_left()
        yield
        ring.middle()
        yield
        ring.end()
        mine = result[c].at[core * 4 + zh]
        for step in (2, 1, 3):
            column[step] = s.along(mine, ZH, step)
        twins.append(s.along(mine, CORE, 1))
        yield
        for step in (1, 3, 2):
            column[step].wait_recv()
            twins.append(s.along(result[c].at[core * 4 + lax.rem(zh + 4 - step, 4)], CORE, 1))
        yield
        for copy in twins:
            copy.wait_recv()

    def own_squares(c):
        start, rows = CUTS[c]
        error = result[c][core * 4 + zh] - blocks[core * 4 + zh, start : start + rows]
        by_row = jnp.sum(error * error, axis=1, keepdims=True)
        row = start + lax.broadcasted_iota(jnp.int32, (rows, TILE), 0)
        column = lax.broadcasted_iota(jnp.int32, (rows, TILE), 1)
        line = jnp.sum(jnp.where((row >> 1) == column, by_row, 0.0), axis=0, keepdims=True)
        return jnp.broadcast_to(line, (8, TILE))

    def exchange(stage, first_slot, those):
        return [
            s.start(squares.at[stage], square_in.at[first_slot + i], peer)
            for i, peer in enumerate(those)
        ]

    def collect(stage, first_slot, copies):
        value = squares[stage]
        for i, copy in enumerate(copies):
            copy.wait_recv()
            value = value + square_in[first_slot + i]
        squares[stage + 1] = value

    columns = [column_steps(c) for c in BOTH]
    reduce, gather = reduce_steps(), gather_steps()

    def go(*those):
        for steps in those:
            next(steps, None)

    z0, z1 = columns
    go(reduce)
    for copy in dec_copies:
        copy.wait()

    @pl.loop(0, CAP)
    def _(k):
        right[k] = stacked_tile(dec_held[k])

    for steps in (reduce, gather):
        for _ in steps:
            pass
    decode()
    go(z0, z1, z0, z1, z0, z1, z0)
    line = own_squares(0)
    go(z1)
    squares[0] = line + own_squares(1)
    copies = exchange(0, 0, plane)
    collect(0, 0, copies)
    copies = exchange(1, 15, stack)
    go(z0, z1)
    collect(1, 15, copies)
    rms[...] = jnp.sqrt(squares[2] * (1.0 / TOTAL_POINTS) + EPSILON)
    go(z0, z1)
    assert s.count == N_SEMS
    s.finish()


def assemble_kernel(result_0, result_1, rms, out, rms_out):
    for i in range(SRC_BLK):
        for (start, rows), part in zip(CUTS, (result_0, result_1)):
            out[i * ROWS + start : i * ROWS + start + rows] = part[i]
    rms_out[...] = rms[0:1, 0:CH]


VMEM = pl.BlockSpec(memory_space=pltpu.VMEM)
HBM = pl.BlockSpec(memory_space=pltpu.HBM)
SMEM = pl.BlockSpec(memory_space=pltpu.SMEM)


def coloured(*lead):
    return [pltpu.VMEM((*lead, rows, TILE), jnp.float32) for _, rows in CUTS]


def body(
    source_field,
    hidden_gain,
    enc_tiles,
    enc_src_block,
    enc_hid_block,
    enc_count,
    dec_tiles,
    dec_src_block,
    dec_hid_block,
    dec_count,
):
    rows = source_field.transpose(0, 2, 1, 3).reshape(SRC_BLK * ROWS, TILE)
    held = pltpu.VMEM((CAP, TILE, TILE), jnp.float32)
    parts = pl.pallas_call(
        whole_kernel,
        out_shape=(
            *coloured(SRC_BLK),
            pltpu.VMEM((8, TILE), jnp.float32),
        ),
        in_specs=[HBM, HBM, SMEM, HBM, HBM, SMEM, HBM, HBM, HBM, HBM],
        out_specs=(VMEM,) * 3,
        scratch_shapes=[
            pltpu.SMEM((CAP,), jnp.int32),
            pltpu.VMEM((1, CAP), jnp.int32),
            pltpu.VMEM((1, CAP), jnp.int32),
            pltpu.SMEM((CAP,), jnp.int32),
            pltpu.VMEM((SRC_BLK * ROWS, TILE), jnp.float32),
            pltpu.VMEM((1, CH), jnp.float32),
            held,
            held,
            pltpu.VMEM((CAP, TILE), jnp.int32),
            pltpu.SMEM((CAP, TILE), jnp.int32),
            pltpu.VMEM((SRC_BLK, ROWS, TILE), jnp.float32),
            pltpu.VMEM((SRC_BLK, ROWS, 2 * TILE), jnp.bfloat16),
            pltpu.VMEM((CAP, 2 * TILE, 2 * TILE), jnp.bfloat16),
            pltpu.VMEM((CAP + 1, ROWS, TILE), jnp.float32),
            coloured(HID_BLK),
            coloured(4, 6),
            coloured(8),
            coloured(4),
            coloured(4),
            coloured(3),
            coloured(HID_BLK),
            coloured(SRC_BLK),
            coloured(4),
            coloured(4),
            [pltpu.VMEM((6, 56, TILE), jnp.float32)] * 2,
            pltpu.VMEM((3, 8, TILE), jnp.float32),
            pltpu.VMEM((30, 8, TILE), jnp.float32),
            pltpu.SemaphoreType.DMA((4, 8)),
            pltpu.SemaphoreType.DMA((N_SEMS,)),
            pltpu.SemaphoreType.DMA((N_SEMS,)),
        ],
        compiler_params=pltpu.CompilerParams(collective_id=0, has_side_effects=True),
    )(
        enc_src_block,
        enc_hid_block.reshape(1, CAP),
        enc_count,
        dec_src_block.reshape(1, CAP),
        dec_hid_block,
        dec_count,
        rows,
        hidden_gain.reshape(1, CH),
        enc_tiles,
        dec_tiles,
    )
    returned, rms = pl.pallas_call(
        assemble_kernel,
        out_shape=(
            jax.ShapeDtypeStruct((SRC_BLK * ROWS, TILE), jnp.float32),
            jax.ShapeDtypeStruct((1, CH), jnp.float32),
        ),
        in_specs=[VMEM] * 3,
        out_specs=(VMEM, VMEM),
    )(*[pltpu.with_memory_space_constraint(part, pltpu.VMEM) for part in parts])
    returned = returned.reshape(SRC_BLK, CH, BATCH, TILE).transpose(0, 2, 1, 3)
    return returned, rms.reshape(CH)


def solution(mesh):
    split = Mesh(mesh.devices.reshape(4, 2, 4, 4, 2), AXES)
    every = P(AXES)
    in_specs = (
        P(SRC, None, None, None),
        P(),
        P(AXES, None, None),
        every,
        every,
        every,
        P(AXES, None, None),
        every,
        every,
        every,
    )
    out_specs = (P(SRC, None, None, None), P())
    return jax.shard_map(body, mesh=split, in_specs=in_specs, out_specs=out_specs, check_vma=False)
```

```python
import jax
import jax.numpy as jnp
from jax import lax
from jax.experimental import pallas as pl
from jax.experimental.pallas import tpu as pltpu
from jax.sharding import Mesh
from jax.sharding import PartitionSpec as P

CH = 98
BATCH = 2
TILE = 128
ROWS = CH * BATCH
SRC_BLK = 8
HID_BLK = 32
CAP = 32
NONE = CAP
TOTAL_POINTS = 256 * BATCH * TILE
EPSILON = 1e-06
AXES = ("src_0", "src_1", "src_2", "hid_0", "hid_1")
SRC = ("src_0", "src_1", "src_2")
SIZES = {"src_0": 4, "src_1": 2, "src_2": 4, "hid_0": 4, "hid_1": 2}
MESH = pl.DeviceIdType.MESH
TILE_DMAS = 2
UNROLL = 16
N_SEMS = 188

X, Z, Y, ZH, CORE = AXES
CUTS = ((0, 96), (96, 100))
HALF = 48
COLOURS = ((X, Y), (Y, X))
BOTH = (0, 1)
ORDER = (2, 1, 3, 0)


def slot_of(block, colour):
    x, z, y = block >> 3, (block >> 2) & 1, block & 3
    if colour == 0:
        return x * 8 + y * 2 + z
    return y * 8 + x * 2 + z


def block_in(slot, colour):
    p, q, z = slot >> 3, (slot >> 1) & 3, slot & 1
    if colour == 0:
        return p * 8 + z * 4 + q
    return q * 8 + z * 4 + p


def split_pair(value):
    high = value.astype(jnp.bfloat16)
    low = (value - high.astype(jnp.float32)).astype(jnp.bfloat16)
    return jnp.concatenate([high, low], axis=1)


def stacked_tile(tile):
    row = split_pair(tile)
    return jnp.concatenate([row, row], axis=0)


def full_product(left, right):
    both = jnp.dot(left, right, preferred_element_type=jnp.float32)
    return both[:, :TILE] + both[:, TILE:]


def tile_copies(tiles, held, sems):
    part = CAP // TILE_DMAS
    return [
        pltpu.make_async_copy(
            tiles.at[pl.ds(i * part, part)], held.at[pl.ds(i * part, part)], sems.at[i]
        )
        for i in range(TILE_DMAS)
    ]


def shifted(axis, step):
    size = SIZES[axis]
    return lax.rem(lax.axis_index(axis) + (step + size), size)


def chain(targets, count):
    row = lax.broadcasted_iota(jnp.int32, (CAP, CAP), 0)
    lane = lax.broadcasted_iota(jnp.int32, (CAP, CAP), 1)
    along = jnp.broadcast_to(targets, (CAP, CAP))
    down = jnp.sum(jnp.where(row == lane, along, 0), axis=1, keepdims=True)
    live = lane < count
    before = jnp.max(jnp.where(live & (lane < row) & (along == down), lane, -1), axis=1, keepdims=True)
    last = jnp.max(jnp.where(live & (along == row), lane, -1), axis=1, keepdims=True)
    return jnp.where(before < 0, NONE, before), jnp.where(last < 0, NONE, last)


class Sender:
    def __init__(self, send_sems, recv_sems):
        self.send_sems, self.recv_sems, self.count, self.sent = send_sems, recv_sems, 0, []

    def start(self, src, dst, where):
        i = self.count
        self.count += 1
        copy = pltpu.make_async_remote_copy(
            src_ref=src,
            dst_ref=dst,
            send_sem=self.send_sems.at[i],
            recv_sem=self.recv_sems.at[i],
            device_id=where,
            device_id_type=MESH,
        )
        copy.start()
        self.sent.append(copy)
        return copy

    def along(self, block, axis, step):
        return self.start(block, block, {axis: shifted(axis, step)})

    def finish(self):
        for copy in self.sent:
            copy.wait_send()


class RingSum:
    def __init__(self, sender, axis, part, landed, total):
        self.s, self.axis, self.part, self.landed, self.total = sender, axis, part, landed, total
        self.right, self.left = {axis: shifted(axis, 1)}, {axis: shifted(axis, -1)}

    def begin_far(self):
        opposite = shifted(self.axis, 2)
        self.r1 = self.s.start(self.part(opposite, 0), self.landed(0), self.right)
        self.l1 = self.s.start(self.part(opposite, 1), self.landed(1), self.left)

    def begin_right(self):
        self.r2 = self.s.start(self.part(self.right[self.axis], 1), self.landed(2), self.right)

    def begin_left(self):
        self.l2 = self.s.start(self.part(self.left[self.axis], 0), self.landed(3), self.left)

    def begin(self):
        self.begin_far()
        self.begin_right()
        self.begin_left()

    def middle_right(self):
        self.r1.wait_recv()
        self.landed(0)[...] = self.landed(0)[...] + self.part(self.right[self.axis], 0)[...]
        self.r3 = self.s.start(self.landed(0), self.landed(4), self.right)

    def middle_left(self):
        self.l1.wait_recv()
        self.landed(1)[...] = self.landed(1)[...] + self.part(self.left[self.axis], 1)[...]
        self.l3 = self.s.start(self.landed(1), self.landed(5), self.left)

    def middle(self):
        self.middle_right()
        self.middle_left()

    def end(self):
        me = lax.axis_index(self.axis)
        landed, part = self.landed, self.part
        self.r2.wait_recv()
        self.l2.wait_recv()
        self.r3.wait_recv()
        self.total(0)[...] = (part(me, 0)[...] + landed(3)[...]) + landed(4)[...]
        self.l3.wait_recv()
        self.total(1)[...] = (part(me, 1)[...] + landed(2)[...]) + landed(5)[...]


def whole_kernel(
    enc_src_any,
    enc_hid_any,
    enc_count,
    dec_src_any,
    dec_hid_any,
    dec_count,
    field_any,
    gain_any,
    enc_tiles,
    dec_tiles,
    result_0,
    result_1,
    rms,
    enc_src,
    enc_hid,
    dec_src,
    dec_hid,
    field,
    gain,
    enc_held,
    dec_held,
    table,
    table_s,
    blocks,
    left,
    right,
    sums,
    partial,
    first_in,
    first_sum,
    pair_in,
    pair_sum,
    second_in,
    hidden,
    back,
    core_in,
    core_sum,
    ring_in,
    squares,
    square_in,
    local_sems,
    send_sems,
    recv_sems,
):
    result = (result_0, result_1)
    x, y, z = lax.axis_index(X), lax.axis_index(Y), lax.axis_index(Z)
    zh, core = lax.axis_index(ZH), lax.axis_index(CORE)
    other, twin = 1 - z, 1 - core
    where = {X: x, Y: y}

    plane = [
        {X: shifted(X, dx), Y: shifted(Y, dy)} for dx in range(4) for dy in range(4) if dx + dy
    ]
    stack = [
        {Z: lax.rem(z + dz, 2), ZH: lax.rem(zh + dh, 4), CORE: lax.rem(core + dc, 2)}
        for dz in range(2)
        for dh in range(4)
        for dc in range(2)
        if dz + dh + dc
    ]
    peers = plane + stack
    barrier = pltpu.get_barrier_semaphore()
    small = [
        pltpu.make_async_copy(there, here, local_sems.at[2, i])
        for i, (there, here) in enumerate(
            (
                (enc_src_any, enc_src),
                (enc_hid_any, enc_hid),
                (dec_src_any, dec_src),
                (dec_hid_any, dec_hid),
                (gain_any, gain),
            )
        )
    ]
    field_copy = pltpu.make_async_copy(field_any, field, local_sems.at[2, 7])
    enc_copies = tile_copies(enc_tiles, enc_held, local_sems.at[0])
    dec_copies = tile_copies(dec_tiles, dec_held, local_sems.at[1])
    for copy in (*small, field_copy, *enc_copies):
        copy.start()
    for peer in peers:
        pl.semaphore_signal(barrier, inc=1, device_id=peer, device_id_type=MESH)

    sums[NONE] = jnp.zeros((ROWS, TILE), jnp.float32)
    for copy in small:
        copy.wait()
    before, last = chain(enc_hid[...] & (HID_BLK - 1), enc_count[0])
    before_back, last_back = chain(dec_src[...] & (SRC_BLK - 1), dec_count[0])
    lane = lax.broadcasted_iota(jnp.int32, (CAP, TILE), 1)
    table[...] = jnp.where(
        lane == 0, before, jnp.where(lane == 1, last, jnp.where(lane == 2, before_back, last_back))
    )
    table_copy = pltpu.make_async_copy(table, table_s, local_sems.at[3, 0])
    field_copy.wait()
    for i in range(SRC_BLK):
        value = field[i * ROWS : (i + 1) * ROWS]
        blocks[i] = value
        left[i] = split_pair(value)
        if i == 1:
            table_copy.start()
    for copy in dec_copies:
        copy.start()
    table_copy.wait()
    for chunk, copy in enumerate(enc_copies):
        copy.wait()

        @pl.loop(0, CAP // TILE_DMAS // UNROLL)
        def _(step, chunk=chunk):
            for i in range(UNROLL):
                k = chunk * (CAP // TILE_DMAS) + step * UNROLL + i
                product = full_product(left[enc_src[k] & (SRC_BLK - 1)], stacked_tile(enc_held[k]))
                sums[k] = sums[table_s[k, 0]] + product

    @pl.loop(0, HID_BLK)
    def _(slot):
        for c in BOTH:
            start, rows = CUTS[c]
            partial[c][slot] = sums[table_s[block_in(slot, c), 1], start : start + rows]

    pl.semaphore_wait(barrier, len(peers))
    s = Sender(send_sems, recv_sems)
    row = lax.broadcasted_iota(jnp.int32, (ROWS, CH), 0)
    column = lax.broadcasted_iota(jnp.int32, (ROWS, CH), 1)
    scale = jnp.sum(
        jnp.where((row >> 1) == column, jnp.broadcast_to(gain[...], (ROWS, CH)), 0.0),
        axis=1,
        keepdims=True,
    )

    def reduce_steps():
        def first_ring(c, i):
            p, q = COLOURS[c]
            there = shifted(q, ORDER[i])
            return RingSum(
                s,
                p,
                lambda m, h: partial[c].at[m * 8 + there * 2 + h],
                lambda n: first_in[c].at[i, n],
                lambda h: first_sum[c].at[there * 2 + h],
            )

        first = [[first_ring(c, i) for i in range(4)] for c in BOTH]
        pairs, second = {}, {}

        def settle(i):
            for c in BOTH:
                first[c][i].end()
                there = shifted(COLOURS[c][1], ORDER[i])
                pairs[c, i] = s.start(
                    first_sum[c].at[there * 2 + other], pair_in[c].at[there], {Z: other}
                )

        def pair_back(c, i):
            there = shifted(COLOURS[c][1], ORDER[i])
            pairs[c, i].wait_recv()
            pair_sum[c][there] = first_sum[c][there * 2 + z] + pair_in[c][there]
            if i < 3:
                second[c, i] = s.start(pair_sum[c].at[there], second_in[c].at[i], {COLOURS[c][1]: there})

        for c in BOTH:
            first[c][0].begin()
        for c in BOTH:
            first[c][1].begin_far()
        yield
        for c in BOTH:
            first[c][0].middle()
            first[c][2].begin_far()
            first[c][1].begin_right()
            first[c][1].begin_left()
        yield
        for c in BOTH:
            first[c][1].middle()
            first[c][3].begin_far()
            first[c][2].begin_right()
            first[c][2].begin_left()
        settle(0)
        yield
        for c in BOTH:
            first[c][2].middle()
            first[c][3].begin_right()
            first[c][3].begin_left()
        settle(1)
        for c in BOTH:
            pair_back(c, 0)
        yield
        for c in BOTH:
            first[c][3].middle()
        settle(2)
        for c in BOTH:
            pair_back(c, 1)
        yield
        settle(3)
        for c in BOTH:
            pair_back(c, 2)
        yield
        evens, odds, values = [], [], []
        for c in BOTH:
            pair_back(c, 3)
            value = pair_sum[c][where[COLOURS[c][1]]]
            for i in range(3):
                second[c, i].wait_recv()
                value = value + second_in[c][i]
            values.append(value)
            parity = lax.broadcasted_iota(jnp.int32, value.shape, 0) & 1
            square = value * value
            evens.append(jnp.sum(jnp.where(parity == 0, square, 0.0), axis=0, keepdims=True))
            odds.append(jnp.sum(jnp.where(parity == 1, square, 0.0), axis=0, keepdims=True))
        even = lax.rsqrt((evens[0] + evens[1]) * (1.0 / CH) + EPSILON)
        odd = lax.rsqrt((odds[0] + odds[1]) * (1.0 / CH) + EPSILON)
        for c in BOTH:
            start, rows = CUTS[c]
            parity = lax.broadcasted_iota(jnp.int32, (rows, TILE), 0) & 1
            p, q = (where[axis] for axis in COLOURS[c])
            hidden[c][p * 8 + q * 2 + z] = (
                values[c] * scale[start : start + rows] * jnp.where(parity == 0, even, odd)
            )

    def gather_steps():
        inner, paired, outer, passed = {}, {}, {}, {}

        def outer_block(c, m, step, far):
            there = shifted(COLOURS[c][1], step)
            return hidden[c].at[m * 8 + there * 2 + (other if far else z)]

        def inner_block(c, step):
            p, q = COLOURS[c]
            return hidden[c].at[where[p] * 8 + shifted(q, step) * 2 + z]

        def to_pair(c, step):
            paired[c, step] = s.along(inner_block(c, step), Z, 1)

        def to_line(c, step, far):
            p = COLOURS[c][0]
            block = outer_block(c, where[p], step, far)
            outer[c, step, far] = [s.along(block, p, 1), s.along(block, p, -1)]

        def along_line(c, step, far):
            p = COLOURS[c][0]
            from_left, from_right = outer[c, step, far]
            if far:
                from_right.wait_recv()
                passed[c, step, far] = s.along(outer_block(c, shifted(p, 1), step, far), p, -1)
            else:
                from_left.wait_recv()
                passed[c, step, far] = s.along(outer_block(c, shifted(p, -1), step, far), p, 1)

        for c in BOTH:
            q, mine = COLOURS[c][1], inner_block(c, 0)
            for step in (1, 3, 2):
                inner[c, step] = s.along(mine, q, step)
            to_pair(c, 0)
        for c in BOTH:
            to_line(c, 0, False)
        yield
        for step in (1, 3, 2):
            for c in BOTH:
                inner[c, step].wait_recv()
                to_pair(c, 4 - step)
                to_line(c, 4 - step, False)
        yield
        for c in BOTH:
            paired[c, 0].wait_recv()
            to_line(c, 0, True)
        yield
        for c in BOTH:
            along_line(c, 0, False)
        yield
        for step in (3, 1, 2):
            for c in BOTH:
                paired[c, step].wait_recv()
                to_line(c, step, True)
        yield
        for step, far in ((3, False), (1, False), (0, True), (2, False), (3, True), (1, True), (2, True)):
            for c in BOTH:
                along_line(c, step, far)
        yield
        for c, step, far in passed:
            outer[c, step, far][0 if far else 1].wait_recv()
            passed[c, step, far].wait_recv()

    def decode():
        for k in range(CAP):
            block = dec_hid[k] & (HID_BLK - 1)
            split = [split_pair(hidden[c][slot_of(block, c)]) for c in BOTH]
            product = full_product(jnp.concatenate(split, axis=0), right[k])
            sums[k] = sums[table_s[k, 2]] + product

        @pl.loop(0, SRC_BLK)
        def _(i):
            for c in BOTH:
                start, rows = CUTS[c]
                back[c][i] = sums[table_s[i, 3], start : start + rows]

    def column_steps(c):
        crossing, column, twins = {}, {}, []
        rows = CUTS[c][1]

        def half_of(block, h):
            return block.at[pl.ds(h * HALF, rows - HALF if h else HALF)]

        ring = RingSum(
            s,
            ZH,
            lambda m, h: half_of(core_sum[c].at[m], h),
            lambda n: ring_in[c].at[n, pl.ds(0, rows - HALF if n in (1, 2, 5) else HALF)],
            lambda h: half_of(result[c].at[core * 4 + zh], h),
        )
        for step in ORDER:
            m = lax.rem(zh + step, 4)
            crossing[step] = s.start(back[c].at[twin * 4 + m], core_in[c].at[m], {CORE: twin})
        yield
        for step in ORDER:
            m = lax.rem(zh + step, 4)
            crossing[step].wait_recv()
            core_sum[c][m] = back[c][core * 4 + m] + core_in[c][m]
            if step == 2:
                ring.begin_far()
            elif step == 1:
                ring.begin_right()
            elif step == 3:
                ring.begin_left()
        yield
        ring.middle()
        yield
        ring.end()
        mine = result[c].at[core * 4 + zh]
        for step in (1, 3, 2):
            column[step] = s.along(mine, ZH, step)
        twins.append(s.along(mine, CORE, 1))
        yield
        for step in (1, 3, 2):
            column[step].wait_recv()
            twins.append(s.along(result[c].at[core * 4 + lax.rem(zh + 4 - step, 4)], CORE, 1))
        yield
        for copy in twins:
            copy.wait_recv()

    def own_squares(c):
        start, rows = CUTS[c]
        error = result[c][core * 4 + zh] - blocks[core * 4 + zh, start : start + rows]
        by_row = jnp.sum(error * error, axis=1, keepdims=True)
        row = start + lax.broadcasted_iota(jnp.int32, (rows, TILE), 0)
        column = lax.broadcasted_iota(jnp.int32, (rows, TILE), 1)
        line = jnp.sum(jnp.where((row >> 1) == column, by_row, 0.0), axis=0, keepdims=True)
        return jnp.broadcast_to(line, (8, TILE))

    def exchange(stage, first_slot, those):
        return [
            s.start(squares.at[stage], square_in.at[first_slot + i], peer)
            for i, peer in enumerate(those)
        ]

    def collect(stage, first_slot, copies):
        value = squares[stage]
        for i, copy in enumerate(copies):
            copy.wait_recv()
            value = value + square_in[first_slot + i]
        squares[stage + 1] = value

    columns = [column_steps(c) for c in BOTH]
    reduce, gather = reduce_steps(), gather_steps()

    def go(*those):
        for steps in those:
            next(steps, None)

    z0, z1 = columns
    go(reduce)
    go(reduce)
    for copy in dec_copies:
        copy.wait()

    @pl.loop(0, CAP)
    def _(k):
        right[k] = stacked_tile(dec_held[k])

    for steps in (reduce, gather):
        for _ in steps:
            pass
    decode()
    go(z0, z1, z0, z1, z0, z1, z0)
    line = own_squares(0)
    go(z1)
    squares[0] = line + own_squares(1)
    copies = exchange(0, 0, plane)
    collect(0, 0, copies)
    copies = exchange(1, 15, stack)
    go(z0, z1)
    collect(1, 15, copies)
    rms[...] = jnp.sqrt(squares[2] * (1.0 / TOTAL_POINTS) + EPSILON)
    go(z0, z1)
    assert s.count == N_SEMS
    s.finish()


def assemble_kernel(result_0, result_1, rms, out, rms_out):
    for i in range(SRC_BLK):
        for (start, rows), part in zip(CUTS, (result_0, result_1)):
            out[i * ROWS + start : i * ROWS + start + rows] = part[i]
    rms_out[...] = rms[0:1, 0:CH]


VMEM = pl.BlockSpec(memory_space=pltpu.VMEM)
HBM = pl.BlockSpec(memory_space=pltpu.HBM)
SMEM = pl.BlockSpec(memory_space=pltpu.SMEM)


def coloured(*lead):
    return [pltpu.VMEM((*lead, rows, TILE), jnp.float32) for _, rows in CUTS]


def body(
    source_field,
    hidden_gain,
    enc_tiles,
    enc_src_block,
    enc_hid_block,
    enc_count,
    dec_tiles,
    dec_src_block,
    dec_hid_block,
    dec_count,
):
    rows = source_field.transpose(0, 2, 1, 3).reshape(SRC_BLK * ROWS, TILE)
    held = pltpu.VMEM((CAP, TILE, TILE), jnp.float32)
    parts = pl.pallas_call(
        whole_kernel,
        out_shape=(
            *coloured(SRC_BLK),
            pltpu.VMEM((8, TILE), jnp.float32),
        ),
        in_specs=[HBM, HBM, SMEM, HBM, HBM, SMEM, HBM, HBM, HBM, HBM],
        out_specs=(VMEM,) * 3,
        scratch_shapes=[
            pltpu.SMEM((CAP,), jnp.int32),
            pltpu.VMEM((1, CAP), jnp.int32),
            pltpu.VMEM((1, CAP), jnp.int32),
            pltpu.SMEM((CAP,), jnp.int32),
            pltpu.VMEM((SRC_BLK * ROWS, TILE), jnp.float32),
            pltpu.VMEM((1, CH), jnp.float32),
            held,
            held,
            pltpu.VMEM((CAP, TILE), jnp.int32),
            pltpu.SMEM((CAP, TILE), jnp.int32),
            pltpu.VMEM((SRC_BLK, ROWS, TILE), jnp.float32),
            pltpu.VMEM((SRC_BLK, ROWS, 2 * TILE), jnp.bfloat16),
            pltpu.VMEM((CAP, 2 * TILE, 2 * TILE), jnp.bfloat16),
            pltpu.VMEM((CAP + 1, ROWS, TILE), jnp.float32),
            coloured(HID_BLK),
            coloured(4, 6),
            coloured(8),
            coloured(4),
            coloured(4),
            coloured(3),
            coloured(HID_BLK),
            coloured(SRC_BLK),
            coloured(4),
            coloured(4),
            [pltpu.VMEM((6, 56, TILE), jnp.float32)] * 2,
            pltpu.VMEM((3, 8, TILE), jnp.float32),
            pltpu.VMEM((30, 8, TILE), jnp.float32),
            pltpu.SemaphoreType.DMA((4, 8)),
            pltpu.SemaphoreType.DMA((N_SEMS,)),
            pltpu.SemaphoreType.DMA((N_SEMS,)),
        ],
        compiler_params=pltpu.CompilerParams(collective_id=0, has_side_effects=True),
    )(
        enc_src_block,
        enc_hid_block.reshape(1, CAP),
        enc_count,
        dec_src_block.reshape(1, CAP),
        dec_hid_block,
        dec_count,
        rows,
        hidden_gain.reshape(1, CH),
        enc_tiles,
        dec_tiles,
    )
    returned, rms = pl.pallas_call(
        assemble_kernel,
        out_shape=(
            jax.ShapeDtypeStruct((SRC_BLK * ROWS, TILE), jnp.float32),
            jax.ShapeDtypeStruct((1, CH), jnp.float32),
        ),
        in_specs=[VMEM] * 3,
        out_specs=(VMEM, VMEM),
    )(*[pltpu.with_memory_space_constraint(part, pltpu.VMEM) for part in parts])
    returned = returned.reshape(SRC_BLK, CH, BATCH, TILE).transpose(0, 2, 1, 3)
    return returned, rms.reshape(CH)


def solution(mesh):
    split = Mesh(mesh.devices.reshape(4, 2, 4, 4, 2), AXES)
    every = P(AXES)
    in_specs = (
        P(SRC, None, None, None),
        P(),
        P(AXES, None, None),
        every,
        every,
        every,
        P(AXES, None, None),
        every,
        every,
        every,
    )
    out_specs = (P(SRC, None, None, None), P())
    return jax.shard_map(body, mesh=split, in_specs=in_specs, out_specs=out_specs, check_vma=False)
```
